256 devices in a mesh: lat: 2 (over x_hi), dp: 64 (over z, y, core), exp: 2 (over x_lo).
Axes of the slice: x: 4 (x_hi: 2, x_lo: 2; x = x_hi * 2 + x_lo), y: 4, z: 8, core: 2. Of those that a mesh axis runs over, the one named last changes fastest.
Arguments:
- images: bfloat16 [128, 32, 256, 192], P(('dp', 'exp'), 'lat'), may hold values from -6 to 6
- cotangent: bfloat16 [128, 32, 256, 192], P(('dp', 'exp'), 'lat'), may hold values from -0.0625 to 0.0625
- labels: int32 [128, 32, 2, 1], P(('dp', 'exp'), 'lat'), may hold values from 0 to 15; in each aligned block of 32 rows (0 to 31, 32 to 63, ..., all dimensions but the last counted through in order) at most 3 rows name the same one
- dw_kernel: float32 [7, 7, 192], replicated, may hold values from -0.875 to 0.875
- ln_gain: float32 [192], replicated, may hold values from 0.5 to 2
- w_expand: bfloat16 [192, 768], replicated, may hold values from -0.4375 to 0.4375
- w_reduce: bfloat16 [768, 192], replicated, may hold values from -0.21875 to 0.21875
- exp_in: bfloat16 [16, 192, 768], P('exp'), may hold values from -0.4375 to 0.4375
- exp_out: bfloat16 [16, 768, 192], P('exp'), may hold values from -0.21875 to 0.21875
Outputs:
- output: bfloat16 [128, 32, 256, 192], P(('dp', 'exp'), 'lat')
- grad_in: float32 [16, 192, 768], P('exp')
- grad_out: float32 [16, 768, 192], P('exp')
The draws below stay inside these ranges and needn't reach their ends.
Inputs may be any that keep to these rules, and one draw needn't show every extreme that they name: `labels`: among the 32 row blocks of one device (aligned runs of 32 blocks in the order clip, row, block), no class is named more than 3 times, a bound that some block reaches.
All inputs are finite; a program needn't handle non-finite values.
Results may differ from the reference program's by a relative error of at most 0.0072.
Values may be sent and summed in bfloat16 or wider, within the bound.
A program may use at most 128 MiB of HBM per device.

```python
import math
import jax
import jax.numpy as jnp
import numpy as np
from jax import lax

C = 192
FF = 768
EXPERTS = 16
W = 256
BLOCK = 128
H = 32
CLIPS = 128
NB = 2
BLK_DEV = 32
CAP = 3
DEVICES = 256


def shard_levels(own_key, dims, shards, low, high):
    def one(position, parts):
        draws = jax.random.uniform(jax.random.fold_in(jax.random.fold_in(own_key, 6), position), (parts,), jnp.float32, low / len(shards), high / len(shards))
        return jnp.repeat(jnp.exp(draws), dims[position] // parts).reshape((-1,) + (1,) * (len(dims) - position - 1))

    level = one(*shards[0])
    for cut in shards[1:]:
        level = level * one(*cut)
    return level


def assign_block(key, own, number, rows, number_of, top, most, skew):
    order = jax.random.permutation(key, number_of)
    packed, ordinary = load_shares(number_of, rows * top, most, skew, True), load_shares(number_of, rows * top, most, skew, False)
    places = jnp.arange(number_of)

    def named(tallies, rotation):
        used = int((tallies > 0).sum())
        fixed = max(1, used // 4)
        shifted = fixed + (places - fixed + rotation * (used - fixed)) % max(1, number_of - fixed)
        return jnp.zeros((number_of,), jnp.int32).at[order[jnp.where(places < fixed, places, shifted)]].set(jnp.asarray(tallies, jnp.int32))

    tallies = jnp.where(number % 4 == 0, named(packed, number // 4), named(ordinary, number - number // 4 - 1))
    mixed = jax.random.permutation(jax.random.fold_in(own, 3), number_of)
    donor, sink = mixed[0:number_of // 2 * 2:2], mixed[1:number_of // 2 * 2:2]
    margin = jnp.minimum(tallies[donor] - 1, most - tallies[sink]) // 2
    margin = jnp.where((donor == order[0]) | (sink == order[0]) | (tallies[sink] == 0), 0, jnp.maximum(margin, 0))
    shifted = jax.random.randint(jax.random.fold_in(own, 4), (number_of // 2,), 0, 1 << 20) % (margin + 1)
    tallies = tallies.at[donor].add(-shifted).at[sink].add(shifted)
    items = jnp.searchsorted(jnp.cumsum(tallies), jnp.arange(rows * top), side="right").astype(jnp.int32)
    table = items.reshape(top, rows).T
    table = table[jax.random.permutation(jax.random.fold_in(own, 1), rows)]
    rotation = jax.random.randint(jax.random.fold_in(own, 2), (rows, 1), 0, top)
    return jnp.take_along_axis(table, (jnp.arange(top)[None, :] + rotation) % top, axis=1)


def load_shares(amount, total, most, skew, full):
    portions = [(1 << 20) // math.isqrt(grade ** skew) + 1 for grade in range(1, amount + 1)]
    largest = most if full else min(most, max(-(-total // amount), total * portions[0] // sum(portions)))
    least = 1 if total - largest >= amount - 1 else 0
    given, surplus = [largest] + [least] * (amount - 1), total - largest - least * (amount - 1)
    while surplus > 0:
        candidates = [i for i in range(1, amount) if given[i] < largest] or [i for i in range(1, amount) if given[i] < most]
        pool, remaining = sum([portions[i] for i in candidates]), surplus
        for i in candidates:
            addition = min(most - given[i], max(1, remaining * portions[i] // pool), surplus)
            given[i] = given[i] + addition
            surplus = surplus - addition
    return np.array(given)


def normal_values(stream_key, extent, scale, reach, shards=(), kind=jnp.bfloat16):
    factor_of = shard_levels(stream_key, extent, shards, -0.22, 0.18) if shards else 1.0
    array = jax.random.normal(stream_key, extent, jnp.float32) * scale * factor_of
    return jnp.minimum(jnp.maximum(array, -reach), reach).astype(kind)


def setup_inputs(seed: int = 0) -> dict:
    streams_of = jax.random.split(jax.random.key(seed), 10)
    images = normal_values(streams_of[0], (CLIPS, H, W, C), 1.0, 6.0, ((0, 128), (1, 2)))
    cotangent = normal_values(streams_of[1], (CLIPS, H, W, C), ((EXPERTS / (CLIPS * H * W)) ** 0.5), 0.0625, ((0, 128), (1, 2)))
    labels_keys = jax.random.split(jax.random.fold_in(streams_of[2], 1), CLIPS * H * NB // BLK_DEV)
    labels_turns = jax.random.permutation(jax.random.fold_in(streams_of[2], 3), CLIPS * H * NB // BLK_DEV)
    labels = jax.vmap(lambda own, number: assign_block(jax.random.fold_in(streams_of[2], 2), own, number, BLK_DEV, EXPERTS, 1, CAP, 2))(labels_keys, labels_turns).reshape((CLIPS, H, NB, 1))
    dw_kernel = normal_values(streams_of[3], (7, 7, C), 49 ** -0.5, 0.875, (), jnp.float32)
    ln_gain = jnp.clip(jnp.exp(jax.random.uniform(streams_of[4], (C,), jnp.float32, math.log(0.5), math.log(2.0))), 0.5, 2.0)
    w_expand = normal_values(streams_of[5], (C, FF), C ** -0.5, 0.4375)
    w_reduce = normal_values(streams_of[6], (FF, C), FF ** -0.5, 0.21875)
    exp_in = normal_values(streams_of[7], (EXPERTS, C, FF), C ** -0.5, 0.4375, ((0, 2),))
    exp_out = normal_values(streams_of[8], (EXPERTS, FF, C), FF ** -0.5, 0.21875, ((0, 2),))
    return {"images": images, "cotangent": cotangent, "labels": labels, "dw_kernel": dw_kernel, "ln_gain": ln_gain, "w_expand": w_expand, "w_reduce": w_reduce, "exp_in": exp_in, "exp_out": exp_out}


def gelu_slope(values):
    return 0.5 * (1.0 + lax.erf(values * 0.7071067811865476)) + values * jnp.exp(-0.5 * values * values) * 0.3989422804014327

def depthwise(padded, kernel):
    row_count = padded.shape[1] - 6
    col_count = padded.shape[2] - 6
    summed = jnp.zeros((padded.shape[0], row_count, col_count, padded.shape[3]), jnp.float32)
    for row_off in range(7):
        for col_off in range(7):
            window = padded[:, row_off:row_off + row_count, col_off:col_off + col_count, :]
            summed = summed + window.astype(jnp.float32) * kernel[row_off, col_off]
    return summed

def dense_block(images, smoothed, ln_gain, w_expand, w_reduce):
    channels = images.shape[-1]
    channel_mean = lax.optimization_barrier(jnp.mean(smoothed, axis=-1, keepdims=True))
    centered = smoothed - channel_mean
    variance = lax.optimization_barrier(jnp.mean(centered * centered, axis=-1, keepdims=True))
    normed = (centered * lax.rsqrt(variance + 1e-06) * ln_gain).astype(jnp.bfloat16)
    flat_normed = normed.reshape(-1, channels)
    expanded = jnp.dot(flat_normed, w_expand, preferred_element_type=jnp.float32)
    active = jax.nn.gelu(expanded, approximate=False).astype(jnp.bfloat16)
    reduced = jnp.dot(active, w_reduce, preferred_element_type=jnp.float32)
    dense_out = images.reshape(-1, channels).astype(jnp.float32) + reduced
    return dense_out.astype(jnp.bfloat16).reshape(images.shape)

def expert_pass(inputs, grads_in, w_in, w_out):
    pre_act = jnp.dot(inputs, w_in, preferred_element_type=jnp.float32)
    hidden = jax.nn.gelu(pre_act, approximate=False).astype(jnp.bfloat16)
    outputs = jnp.dot(hidden, w_out, preferred_element_type=jnp.float32).astype(jnp.bfloat16)
    grad_out = jnp.dot(hidden.T, grads_in, preferred_element_type=jnp.float32)
    back_prop = jnp.dot(grads_in, w_out.T, preferred_element_type=jnp.float32)
    scaled = (back_prop * gelu_slope(pre_act)).astype(jnp.bfloat16)
    grad_in = jnp.dot(inputs.T, scaled, preferred_element_type=jnp.float32)
    return (outputs, grad_in, grad_out)

def reference(images, cotangent, labels, dw_kernel, ln_gain, w_expand, w_reduce, exp_in, exp_out):
    channels = images.shape[-1]

    def one_image(picture):
        padded = jnp.pad(picture[None], ((0, 0), (3, 3), (3, 3), (0, 0)))
        return dense_block(picture[None], depthwise(padded, dw_kernel), ln_gain, w_expand, w_reduce)[0]
    dense_out = lax.map(one_image, images)
    blocks = dense_out.reshape(-1, BLOCK * channels)
    grad_blocks = cotangent.reshape(-1, BLOCK * channels)
    flat_labels = labels.reshape(-1).astype(jnp.int32)
    most_blocks = DEVICES * CAP

    def per_expert(gathered_out, expert):
        member = flat_labels == expert
        chosen = jnp.nonzero(member, size=most_blocks, fill_value=0)[0].astype(jnp.int32)
        live_count = jnp.sum(member.astype(jnp.int32))
        is_live = (jnp.arange(most_blocks, dtype=jnp.int32) < live_count)[:, None]
        inputs = blocks[chosen].reshape(-1, channels)
        grads_in = jnp.where(is_live, grad_blocks[chosen], jnp.zeros((), jnp.bfloat16)).reshape(-1, channels)
        outputs, grad_in, grad_out = expert_pass(inputs, grads_in, exp_in[expert], exp_out[expert])
        outputs = jnp.where(is_live, outputs.reshape(most_blocks, -1), jnp.zeros((), jnp.bfloat16))
        gathered_out = gathered_out.at[chosen].add(outputs)
        return (gathered_out, (grad_in, grad_out))
    empty_out = jnp.zeros(blocks.shape, jnp.bfloat16)
    expert_out, grads = lax.scan(per_expert, empty_out, jnp.arange(EXPERTS, dtype=jnp.int32))
    output = (dense_out.astype(jnp.float32) + expert_out.reshape(dense_out.shape).astype(jnp.float32)).astype(jnp.bfloat16)
    return (output, grads[0], grads[1])
```

```python
import jax
import jax.numpy as jnp
from jax import lax
from jax.sharding import PartitionSpec as P

EXPERTS = 16
BLOCK = 128
CAP = 3


def with_halo(block, sides, width):
    for axis, dim in sides:
        count = lax.axis_size(axis)
        forward = [(i, i + 1) for i in range(count - 1)]
        backward = [(target, source) for source, target in forward]
        low = lax.ppermute(
            lax.slice_in_dim(block, block.shape[dim] - width, None, axis=dim), axis, forward
        )
        high = lax.ppermute(lax.slice_in_dim(block, 0, width, axis=dim), axis, backward)
        block = jnp.concatenate([low, block, high], axis=dim)
    return block


def gelu_slope(values):
    return (
        0.5 * (1.0 + lax.erf(values * 0.7071067811865476))
        + values * jnp.exp(-0.5 * values * values) * 0.3989422804014327
    )


def depthwise(padded, kernel):
    row_count = padded.shape[1] - 6
    col_count = padded.shape[2] - 6
    summed = jnp.zeros((padded.shape[0], row_count, col_count, padded.shape[3]), jnp.float32)
    for row_off in range(7):
        for col_off in range(7):
            window = padded[:, row_off : row_off + row_count, col_off : col_off + col_count, :]
            summed = summed + window.astype(jnp.float32) * kernel[row_off, col_off]
    return summed


def widen(picture):
    return jnp.pad(picture, ((0, 0), (0, 0), (3, 3), (0, 0)))


def dense_block(images, smoothed, ln_gain, w_expand, w_reduce):
    channels = images.shape[-1]
    channel_mean = jnp.mean(smoothed, axis=-1, keepdims=True)
    centered = smoothed - channel_mean
    variance = jnp.mean(centered * centered, axis=-1, keepdims=True)
    normed = (centered * lax.rsqrt(variance + 1e-06) * ln_gain).astype(jnp.bfloat16)
    flat_normed = normed.reshape(-1, channels)
    expanded = jnp.dot(flat_normed, w_expand, preferred_element_type=jnp.float32)
    active = jax.nn.gelu(expanded, approximate=False).astype(jnp.bfloat16)
    reduced = jnp.dot(active, w_reduce, preferred_element_type=jnp.float32)
    dense_out = images.reshape(-1, channels).astype(jnp.float32) + reduced
    return dense_out.astype(jnp.bfloat16).reshape(images.shape)


def expert_pass(inputs, grads_in, w_in, w_out):
    pre_act = jnp.dot(inputs, w_in, preferred_element_type=jnp.float32)
    hidden = jax.nn.gelu(pre_act, approximate=False).astype(jnp.bfloat16)
    outputs = jnp.dot(hidden, w_out, preferred_element_type=jnp.float32).astype(jnp.bfloat16)
    grad_out = jnp.dot(hidden.T, grads_in, preferred_element_type=jnp.float32)
    back_prop = jnp.dot(grads_in, w_out.T, preferred_element_type=jnp.float32)
    scaled = (back_prop * gelu_slope(pre_act)).astype(jnp.bfloat16)
    grad_in = jnp.dot(inputs.T, scaled, preferred_element_type=jnp.float32)
    return (outputs, grad_in, grad_out)


def body(images, cotangent, labels, dw_kernel, ln_gain, w_expand, w_reduce, exp_in, exp_out):
    channels = images.shape[-1]
    padded = with_halo(images, (("lat", 1),), 3)
    smoothed = depthwise(widen(padded), dw_kernel)
    dense_out = dense_block(images, smoothed, ln_gain, w_expand, w_reduce)
    block_width = BLOCK * channels
    blocks = dense_out.reshape(-1, block_width)
    grad_blocks = cotangent.reshape(-1, block_width)
    flat_labels = labels.reshape(-1)
    members = (flat_labels[:, None] == jnp.arange(EXPERTS, dtype=jnp.int32)[None, :]).astype(
        jnp.int32
    )
    before = jnp.sum(jnp.cumsum(members, axis=0) * members, axis=1) - 1
    slot_of = flat_labels * CAP + before
    placer = (jnp.arange(EXPERTS * CAP, dtype=jnp.int32)[:, None] == slot_of[None, :]).astype(
        jnp.bfloat16
    )
    outgoing = (
        jnp.dot(placer, blocks, preferred_element_type=jnp.float32)
        .astype(jnp.bfloat16)
        .reshape(EXPERTS, CAP, block_width)
    )
    outgoing_grads = (
        jnp.dot(placer, grad_blocks, preferred_element_type=jnp.float32)
        .astype(jnp.bfloat16)
        .reshape(EXPERTS, CAP, block_width)
    )

    def run_expert(expert_items):
        inputs, grads_in, w_in, w_out = expert_items
        outputs, grad_in, grad_out = expert_pass(
            inputs.reshape(-1, channels), grads_in.reshape(-1, channels), w_in, w_out
        )
        return (outputs.reshape(inputs.shape), grad_in, grad_out)

    arrived, arrived_grads = (
        lax.all_to_all(outgoing, "exp", split_axis=0, concat_axis=1, tiled=True),
        lax.all_to_all(outgoing_grads, "exp", split_axis=0, concat_axis=1, tiled=True),
    )
    results, grad_in, grad_out = lax.map(run_expert, (arrived, arrived_grads, exp_in, exp_out))
    returned = lax.all_to_all(results, "exp", split_axis=1, concat_axis=0, tiled=True)
    grad_in, grad_out = lax.psum(lax.psum((grad_in, grad_out), "dp"), "lat")
    expert_out = jnp.dot(
        placer.T, returned.reshape(EXPERTS * CAP, block_width), preferred_element_type=jnp.float32
    ).astype(jnp.bfloat16)
    output = (
        dense_out.astype(jnp.float32) + expert_out.reshape(dense_out.shape).astype(jnp.float32)
    ).astype(jnp.bfloat16)
    return (output, grad_in, grad_out)


def solution(mesh):
    in_specs = (
        P(("dp", "exp"), "lat", None, None),
        P(("dp", "exp"), "lat", None, None),
        P(("dp", "exp"), "lat", None, None),
        P(),
        P(),
        P(),
        P(),
        P("exp", None, None),
        P("exp", None, None),
    )
    out_specs = (P(("dp", "exp"), "lat", None, None), P("exp", None, None), P("exp", None, None))
    return jax.shard_map(body, mesh=mesh, in_specs=in_specs, out_specs=out_specs, check_vma=False)
```

```python
import jax
import jax.numpy as jnp
from jax import lax
from jax.sharding import PartitionSpec as P
from jax.experimental import pallas as pl
from jax.experimental.pallas import tpu as pltpu

EXPERTS = 16
BLOCK = 128
CAP = 3


def with_halo(block, sides, width):
    for axis, dim in sides:
        count = lax.axis_size(axis)
        forward = [(i, i + 1) for i in range(count - 1)]
        backward = [(target, source) for source, target in forward]
        low = lax.ppermute(
            lax.slice_in_dim(block, block.shape[dim] - width, None, axis=dim), axis, forward
        )
        high = lax.ppermute(lax.slice_in_dim(block, 0, width, axis=dim), axis, backward)
        block = jnp.concatenate([low, block, high], axis=dim)
    return block


def reduce_plan(lat_size, dp_size):
    dp_bits = dp_size.bit_length() - 1
    rest = list(range(1, dp_bits))
    other = rest[2:] + rest[:2] if len(rest) > 2 else rest
    plan = [("dp", 0, 0)] + [("dp", a, b) for a, b in zip(rest, other)]
    plan += [("lat", 0, 0)] * (lat_size.bit_length() - 1)
    return plan


def allreduce_kernel(plan, rows, in_ref, out_ref, *scratch):
    stages = len(plan)
    bufs = scratch[:stages]
    sums = scratch[stages:2 * stages]
    rs_send, rs_recv, ag_send, ag_recv = scratch[2 * stages:]
    lat = lax.axis_index("lat")
    dp = lax.axis_index("dp")
    ex = lax.axis_index("exp")
    core = dp % 2

    bits, partners = [], []
    for axis, b0, b1 in plan:
        me = dp if axis == "dp" else lat
        bit = jnp.where(core == 0, (me // (1 << b0)) % 2, (me // (1 << b1)) % 2)
        step = jnp.where(core == 0, 1 << b0, 1 << b1)
        other = me + (1 - 2 * bit) * step
        bits.append(bit)
        partners.append((lat, other, ex) if axis == "dp" else (other, dp, ex))

    barrier = pltpu.get_barrier_semaphore()
    for dev in partners:
        pl.semaphore_signal(barrier, 1, device_id=dev, device_id_type=pl.DeviceIdType.MESH)
    pl.semaphore_wait(barrier, stages)

    los = []
    lo = jnp.int32(0)
    for k in range(stages):
        half = rows >> (k + 1)
        los.append(lo)
        src = in_ref if k == 0 else sums[k - 1]
        keep = bits[k] * half
        give = (1 - bits[k]) * half
        copy = pltpu.make_async_remote_copy(
            src_ref=src.at[pl.ds(give, half)],
            dst_ref=bufs[k],
            send_sem=rs_send.at[k],
            recv_sem=rs_recv.at[k],
            device_id=partners[k],
            device_id_type=pl.DeviceIdType.MESH,
        )
        copy.start()
        copy.wait()
        chunk = min(half, 1152)

        def add(i, carry, src=src, keep=keep, chunk=chunk, k=k):
            at = pl.multiple_of(i * chunk, 8)
            sums[k][pl.ds(at, chunk)] = src[pl.ds(keep + at, chunk)] + bufs[k][pl.ds(at, chunk)]
            return carry

        lax.fori_loop(0, half // chunk, add, 0)
        lo = lo + bits[k] * half

    last = rows >> stages
    out_ref[pl.ds(lo, last)] = sums[stages - 1][...]
    for k in reversed(range(stages)):
        half = rows >> (k + 1)
        copy = pltpu.make_async_remote_copy(
            src_ref=out_ref.at[pl.ds(lo, half)],
            dst_ref=out_ref.at[pl.ds(lo, half)],
            send_sem=ag_send.at[k],
            recv_sem=ag_recv.at[k],
            device_id=partners[k],
            device_id_type=pl.DeviceIdType.MESH,
        )
        copy.start()
        copy.wait()
        lo = los[k]


def tree_allreduce(flat):
    rows = flat.shape[0]
    plan = reduce_plan(lax.axis_size("lat"), lax.axis_size("dp"))
    stages = len(plan)
    scratch = [pltpu.VMEM((rows >> (k + 1), 128), jnp.float32) for k in range(stages)] * 2
    scratch += [pltpu.SemaphoreType.DMA((stages,))] * 4
    return pl.pallas_call(
        lambda *refs: allreduce_kernel(plan, rows, *refs),
        out_shape=jax.ShapeDtypeStruct(flat.shape, flat.dtype),
        in_specs=[pl.BlockSpec(memory_space=pltpu.VMEM)],
        out_specs=pl.BlockSpec(memory_space=pltpu.VMEM),
        scratch_shapes=scratch,
        compiler_params=pltpu.CompilerParams(
            collective_id=0, has_side_effects=True, vmem_limit_bytes=62 * 1024 * 1024
        ),
    )(flat)

def gelu_slope(values):
    return (
        0.5 * (1.0 + lax.erf(values * 0.7071067811865476))
        + values * jnp.exp(-0.5 * values * values) * 0.3989422804014327
    )


def depthwise(padded, kernel):
    row_count = padded.shape[1] - 6
    col_count = padded.shape[2] - 6
    summed = jnp.zeros((padded.shape[0], row_count, col_count, padded.shape[3]), jnp.float32)
    for row_off in range(7):
        for col_off in range(7):
            window = padded[:, row_off : row_off + row_count, col_off : col_off + col_count, :]
            summed = summed + window.astype(jnp.float32) * kernel[row_off, col_off]
    return summed


def widen(picture):
    return jnp.pad(picture, ((0, 0), (0, 0), (3, 3), (0, 0)))


def dense_block(images, smoothed, ln_gain, w_expand, w_reduce):
    channels = images.shape[-1]
    channel_mean = jnp.mean(smoothed, axis=-1, keepdims=True)
    centered = smoothed - channel_mean
    variance = jnp.mean(centered * centered, axis=-1, keepdims=True)
    normed = (centered * lax.rsqrt(variance + 1e-06) * ln_gain).astype(jnp.bfloat16)
    flat_normed = normed.reshape(-1, channels)
    expanded = jnp.dot(flat_normed, w_expand, preferred_element_type=jnp.float32)
    active = jax.nn.gelu(expanded, approximate=False).astype(jnp.bfloat16)
    reduced = jnp.dot(active, w_reduce, preferred_element_type=jnp.float32)
    dense_out = images.reshape(-1, channels).astype(jnp.float32) + reduced
    return dense_out.astype(jnp.bfloat16).reshape(images.shape)


def expert_pass(inputs, grads_in, w_in, w_out):
    pre_act = jnp.dot(inputs, w_in, preferred_element_type=jnp.float32)
    hidden = jax.nn.gelu(pre_act, approximate=False).astype(jnp.bfloat16)
    outputs = jnp.dot(hidden, w_out, preferred_element_type=jnp.float32).astype(jnp.bfloat16)
    grad_out = jnp.dot(hidden.T, grads_in, preferred_element_type=jnp.float32)
    back_prop = jnp.dot(grads_in, w_out.T, preferred_element_type=jnp.float32)
    scaled = (back_prop * gelu_slope(pre_act)).astype(jnp.bfloat16)
    grad_in = jnp.dot(inputs.T, scaled, preferred_element_type=jnp.float32)
    return (outputs, grad_in, grad_out)


def body(images, cotangent, labels, dw_kernel, ln_gain, w_expand, w_reduce, exp_in, exp_out):
    channels = images.shape[-1]
    padded = with_halo(images, (("lat", 1),), 3)
    smoothed = depthwise(widen(padded), dw_kernel)
    dense_out = dense_block(images, smoothed, ln_gain, w_expand, w_reduce)
    block_width = BLOCK * channels
    blocks = dense_out.reshape(-1, block_width)
    grad_blocks = cotangent.reshape(-1, block_width)
    flat_labels = labels.reshape(-1)
    members = (flat_labels[:, None] == jnp.arange(EXPERTS, dtype=jnp.int32)[None, :]).astype(
        jnp.int32
    )
    before = jnp.sum(jnp.cumsum(members, axis=0) * members, axis=1) - 1
    slot_of = flat_labels * CAP + before
    placer = (jnp.arange(EXPERTS * CAP, dtype=jnp.int32)[:, None] == slot_of[None, :]).astype(
        jnp.bfloat16
    )
    outgoing = (
        jnp.dot(placer, blocks, preferred_element_type=jnp.float32)
        .astype(jnp.bfloat16)
        .reshape(EXPERTS, CAP, block_width)
    )
    outgoing_grads = (
        jnp.dot(placer, grad_blocks, preferred_element_type=jnp.float32)
        .astype(jnp.bfloat16)
        .reshape(EXPERTS, CAP, block_width)
    )

    def run_expert(expert_items):
        inputs, grads_in, w_in, w_out = expert_items
        outputs, grad_in, grad_out = expert_pass(
            inputs.reshape(-1, channels), grads_in.reshape(-1, channels), w_in, w_out
        )
        return (outputs.reshape(inputs.shape), grad_in, grad_out)

    arrived, arrived_grads = (
        lax.all_to_all(outgoing, "exp", split_axis=0, concat_axis=1, tiled=True),
        lax.all_to_all(outgoing_grads, "exp", split_axis=0, concat_axis=1, tiled=True),
    )
    results, grad_in, grad_out = lax.map(run_expert, (arrived, arrived_grads, exp_in, exp_out))
    returned = lax.all_to_all(results, "exp", split_axis=1, concat_axis=0, tiled=True)
    flat = jnp.concatenate([grad_in.reshape(-1, 128), grad_out.reshape(-1, 128)])
    flat = tree_allreduce(flat)
    half = flat.shape[0] // 2
    grad_in = flat[:half].reshape(grad_in.shape)
    grad_out = flat[half:].reshape(grad_out.shape)
    expert_out = jnp.dot(
        placer.T, returned.reshape(EXPERTS * CAP, block_width), preferred_element_type=jnp.float32
    ).astype(jnp.bfloat16)
    output = (
        dense_out.astype(jnp.float32) + expert_out.reshape(dense_out.shape).astype(jnp.float32)
    ).astype(jnp.bfloat16)
    return (output, grad_in, grad_out)


def solution(mesh):
    in_specs = (
        P(("dp", "exp"), "lat", None, None),
        P(("dp", "exp"), "lat", None, None),
        P(("dp", "exp"), "lat", None, None),
        P(),
        P(),
        P(),
        P(),
        P("exp", None, None),
        P("exp", None, None),
    )
    out_specs = (P(("dp", "exp"), "lat", None, None), P("exp", None, None), P("exp", None, None))
    return jax.shard_map(body, mesh=mesh, in_specs=in_specs, out_specs=out_specs, check_vma=False)
```

```python
import jax
import jax.numpy as jnp
from jax import lax
from jax.sharding import PartitionSpec as P
from jax.experimental import pallas as pl
from jax.experimental.pallas import tpu as pltpu

EXPERTS = 16
BLOCK = 128
CAP = 3


def with_halo(block, sides, width):
    for axis, dim in sides:
        count = lax.axis_size(axis)
        forward = [(i, i + 1) for i in range(count - 1)]
        backward = [(target, source) for source, target in forward]
        low = lax.ppermute(
            lax.slice_in_dim(block, block.shape[dim] - width, None, axis=dim), axis, forward
        )
        high = lax.ppermute(lax.slice_in_dim(block, 0, width, axis=dim), axis, backward)
        block = jnp.concatenate([low, block, high], axis=dim)
    return block


def reduce_plan(lat_size, dp_size):
    dp_bits = dp_size.bit_length() - 1
    rest = list(range(1, dp_bits))
    other = rest[2:] + rest[:2] if len(rest) > 2 else rest
    plan = [("dp", 0, 0)] + [("dp", a, b) for a, b in zip(rest, other)]
    plan += [("lat", 0, 0)] * (lat_size.bit_length() - 1)
    return plan


def allreduce_kernel(plan, rows, in_ref, out_ref, *scratch):
    stages = len(plan)
    bufs = scratch[:stages]
    sums = scratch[stages:2 * stages]
    staged = scratch[2 * stages:3 * stages]
    gathered = scratch[3 * stages]
    rs_send, rs_recv, ag_send, ag_recv = scratch[3 * stages + 1:]
    lat = lax.axis_index("lat")
    dp = lax.axis_index("dp")
    ex = lax.axis_index("exp")
    core = dp % 2

    bits, partners = [], []
    for axis, b0, b1 in plan:
        me = dp if axis == "dp" else lat
        bit = jnp.where(core == 0, (me // (1 << b0)) % 2, (me // (1 << b1)) % 2)
        step = jnp.where(core == 0, 1 << b0, 1 << b1)
        other = me + (1 - 2 * bit) * step
        bits.append(bit)
        partners.append((lat, other, ex) if axis == "dp" else (other, dp, ex))

    barrier = pltpu.get_barrier_semaphore()
    for dev in partners:
        pl.semaphore_signal(barrier, 1, device_id=dev, device_id_type=pl.DeviceIdType.MESH)
    pl.semaphore_wait(barrier, stages)

    def chunked(count, body):
        chunk = min(count, 1152)
        lax.fori_loop(0, count // chunk, lambda i, c: (body(pl.multiple_of(i * chunk, 16), chunk), c)[1], 0)

    los = []
    lo = jnp.int32(0)
    for k in range(stages):
        half = rows >> (k + 1)
        los.append(lo)
        src = in_ref if k == 0 else sums[k - 1]
        keep = bits[k] * half
        give = (1 - bits[k]) * half

        def narrow(at, chunk, src=src, give=give, k=k):
            staged[k][pl.ds(at, chunk)] = src[pl.ds(pl.multiple_of(give + at, 16), chunk)].astype(jnp.bfloat16)

        chunked(half, narrow)
        copy = pltpu.make_async_remote_copy(
            src_ref=staged[k],
            dst_ref=bufs[k],
            send_sem=rs_send.at[k],
            recv_sem=rs_recv.at[k],
            device_id=partners[k],
            device_id_type=pl.DeviceIdType.MESH,
        )
        copy.start()
        copy.wait()

        def add(at, chunk, src=src, keep=keep, k=k):
            sums[k][pl.ds(at, chunk)] = src[pl.ds(pl.multiple_of(keep + at, 16), chunk)] + bufs[k][
                pl.ds(at, chunk)
            ].astype(jnp.float32)

        chunked(half, add)
        lo = lo + bits[k] * half

    last = rows >> stages
    lo = pl.multiple_of(lo, 16)
    gathered[pl.ds(lo, last)] = sums[stages - 1][...].astype(jnp.bfloat16)
    for k in reversed(range(stages)):
        half = rows >> (k + 1)
        copy = pltpu.make_async_remote_copy(
            src_ref=gathered.at[pl.ds(pl.multiple_of(lo, 16), half)],
            dst_ref=gathered.at[pl.ds(pl.multiple_of(lo, 16), half)],
            send_sem=ag_send.at[k],
            recv_sem=ag_recv.at[k],
            device_id=partners[k],
            device_id_type=pl.DeviceIdType.MESH,
        )
        copy.start()
        copy.wait()
        lo = los[k]

    def widen_out(at, chunk):
        out_ref[pl.ds(at, chunk)] = gathered[pl.ds(at, chunk)].astype(jnp.float32)

    chunked(rows, widen_out)


def tree_allreduce(flat):
    rows = flat.shape[0]
    plan = reduce_plan(lax.axis_size("lat"), lax.axis_size("dp"))
    stages = len(plan)
    scratch = [pltpu.VMEM((rows >> (k + 1), 128), jnp.bfloat16) for k in range(stages)]
    scratch += [pltpu.VMEM((rows >> (k + 1), 128), jnp.float32) for k in range(stages)]
    scratch += [pltpu.VMEM((rows >> (k + 1), 128), jnp.bfloat16) for k in range(stages)]
    scratch += [pltpu.VMEM((rows, 128), jnp.bfloat16)]
    scratch += [pltpu.SemaphoreType.DMA((stages,))] * 4
    return pl.pallas_call(
        lambda *refs: allreduce_kernel(plan, rows, *refs),
        out_shape=jax.ShapeDtypeStruct(flat.shape, flat.dtype),
        in_specs=[pl.BlockSpec(memory_space=pltpu.VMEM)],
        out_specs=pl.BlockSpec(memory_space=pltpu.VMEM),
        scratch_shapes=scratch,
        compiler_params=pltpu.CompilerParams(
            collective_id=0, has_side_effects=True, vmem_limit_bytes=62 * 1024 * 1024
        ),
    )(flat)

def gelu_slope(values):
    return (
        0.5 * (1.0 + lax.erf(values * 0.7071067811865476))
        + values * jnp.exp(-0.5 * values * values) * 0.3989422804014327
    )


def depthwise(padded, kernel):
    row_count = padded.shape[1] - 6
    col_count = padded.shape[2] - 6
    summed = jnp.zeros((padded.shape[0], row_count, col_count, padded.shape[3]), jnp.float32)
    for row_off in range(7):
        for col_off in range(7):
            window = padded[:, row_off : row_off + row_count, col_off : col_off + col_count, :]
            summed = summed + window.astype(jnp.float32) * kernel[row_off, col_off]
    return summed


def widen(picture):
    return jnp.pad(picture, ((0, 0), (0, 0), (3, 3), (0, 0)))


def dense_block(images, smoothed, ln_gain, w_expand, w_reduce):
    channels = images.shape[-1]
    channel_mean = jnp.mean(smoothed, axis=-1, keepdims=True)
    centered = smoothed - channel_mean
    variance = jnp.mean(centered * centered, axis=-1, keepdims=True)
    normed = (centered * lax.rsqrt(variance + 1e-06) * ln_gain).astype(jnp.bfloat16)
    flat_normed = normed.reshape(-1, channels)
    expanded = jnp.dot(flat_normed, w_expand, preferred_element_type=jnp.float32)
    active = jax.nn.gelu(expanded, approximate=False).astype(jnp.bfloat16)
    reduced = jnp.dot(active, w_reduce, preferred_element_type=jnp.float32)
    dense_out = images.reshape(-1, channels).astype(jnp.float32) + reduced
    return dense_out.astype(jnp.bfloat16).reshape(images.shape)


def expert_pass(inputs, grads_in, w_in, w_out):
    pre_act = jnp.dot(inputs, w_in, preferred_element_type=jnp.float32)
    hidden = jax.nn.gelu(pre_act, approximate=False).astype(jnp.bfloat16)
    outputs = jnp.dot(hidden, w_out, preferred_element_type=jnp.float32).astype(jnp.bfloat16)
    grad_out = jnp.dot(hidden.T, grads_in, preferred_element_type=jnp.float32)
    back_prop = jnp.dot(grads_in, w_out.T, preferred_element_type=jnp.float32)
    scaled = (back_prop * gelu_slope(pre_act)).astype(jnp.bfloat16)
    grad_in = jnp.dot(inputs.T, scaled, preferred_element_type=jnp.float32)
    return (outputs, grad_in, grad_out)


def body(images, cotangent, labels, dw_kernel, ln_gain, w_expand, w_reduce, exp_in, exp_out):
    channels = images.shape[-1]
    padded = with_halo(images, (("lat", 1),), 3)
    smoothed = depthwise(widen(padded), dw_kernel)
    dense_out = dense_block(images, smoothed, ln_gain, w_expand, w_reduce)
    block_width = BLOCK * channels
    blocks = dense_out.reshape(-1, block_width)
    grad_blocks = cotangent.reshape(-1, block_width)
    flat_labels = labels.reshape(-1)
    members = (flat_labels[:, None] == jnp.arange(EXPERTS, dtype=jnp.int32)[None, :]).astype(
        jnp.int32
    )
    before = jnp.sum(jnp.cumsum(members, axis=0) * members, axis=1) - 1
    slot_of = flat_labels * CAP + before
    placer = (jnp.arange(EXPERTS * CAP, dtype=jnp.int32)[:, None] == slot_of[None, :]).astype(
        jnp.bfloat16
    )
    outgoing = (
        jnp.dot(placer, blocks, preferred_element_type=jnp.float32)
        .astype(jnp.bfloat16)
        .reshape(EXPERTS, CAP, block_width)
    )
    outgoing_grads = (
        jnp.dot(placer, grad_blocks, preferred_element_type=jnp.float32)
        .astype(jnp.bfloat16)
        .reshape(EXPERTS, CAP, block_width)
    )

    def run_expert(expert_items):
        inputs, grads_in, w_in, w_out = expert_items
        outputs, grad_in, grad_out = expert_pass(
            inputs.reshape(-1, channels), grads_in.reshape(-1, channels), w_in, w_out
        )
        return (outputs.reshape(inputs.shape), grad_in, grad_out)

    arrived, arrived_grads = (
        lax.all_to_all(outgoing, "exp", split_axis=0, concat_axis=1, tiled=True),
        lax.all_to_all(outgoing_grads, "exp", split_axis=0, concat_axis=1, tiled=True),
    )
    results, grad_in, grad_out = lax.map(run_expert, (arrived, arrived_grads, exp_in, exp_out))
    returned = lax.all_to_all(results, "exp", split_axis=1, concat_axis=0, tiled=True)
    flat = jnp.concatenate([grad_in.reshape(-1, 128), grad_out.reshape(-1, 128)])
    flat = tree_allreduce(flat)
    half = flat.shape[0] // 2
    grad_in = flat[:half].reshape(grad_in.shape)
    grad_out = flat[half:].reshape(grad_out.shape)
    expert_out = jnp.dot(
        placer.T, returned.reshape(EXPERTS * CAP, block_width), preferred_element_type=jnp.float32
    ).astype(jnp.bfloat16)
    output = (
        dense_out.astype(jnp.float32) + expert_out.reshape(dense_out.shape).astype(jnp.float32)
    ).astype(jnp.bfloat16)
    return (output, grad_in, grad_out)


def solution(mesh):
    in_specs = (
        P(("dp", "exp"), "lat", None, None),
        P(("dp", "exp"), "lat", None, None),
        P(("dp", "exp"), "lat", None, None),
        P(),
        P(),
        P(),
        P(),
        P("exp", None, None),
        P("exp", None, None),
    )
    out_specs = (P(("dp", "exp"), "lat", None, None), P("exp", None, None), P("exp", None, None))
    return jax.shard_map(body, mesh=mesh, in_specs=in_specs, out_specs=out_specs, check_vma=False)
```

```python
import jax
import jax.numpy as jnp
from jax import lax
from jax.sharding import PartitionSpec as P
from jax.experimental import pallas as pl
from jax.experimental.pallas import tpu as pltpu

EXPERTS = 16
BLOCK = 128
CAP = 3


def with_halo(block, sides, width):
    for axis, dim in sides:
        count = lax.axis_size(axis)
        forward = [(i, i + 1) for i in range(count - 1)]
        backward = [(target, source) for source, target in forward]
        low = lax.ppermute(
            lax.slice_in_dim(block, block.shape[dim] - width, None, axis=dim), axis, forward
        )
        high = lax.ppermute(lax.slice_in_dim(block, 0, width, axis=dim), axis, backward)
        block = jnp.concatenate([low, block, high], axis=dim)
    return block


def reduce_plan(lat_size, dp_size):
    dp_bits = dp_size.bit_length() - 1
    rest = list(range(1, dp_bits))
    other = rest[2:] + rest[:2] if len(rest) > 2 else rest
    plan = [("dp", 0, 0)] + [("dp", a, b) for a, b in zip(rest, other)]
    plan += [("lat", 0, 0)] * (lat_size.bit_length() - 1)
    return plan


def allreduce_kernel(plan, rows, in_ref, out_in, out_outt, *scratch):
    stages = len(plan)
    bufs = scratch[:stages]
    sums = scratch[stages:2 * stages]
    staged = scratch[2 * stages:3 * stages]
    gathered = scratch[3 * stages]
    rs_send, rs_recv, ag_send, ag_recv = scratch[3 * stages + 1:]
    lat = lax.axis_index("lat")
    dp = lax.axis_index("dp")
    ex = lax.axis_index("exp")
    core = dp % 2

    bits, partners = [], []
    for axis, b0, b1 in plan:
        me = dp if axis == "dp" else lat
        bit = jnp.where(core == 0, (me // (1 << b0)) % 2, (me // (1 << b1)) % 2)
        step = jnp.where(core == 0, 1 << b0, 1 << b1)
        other = me + (1 - 2 * bit) * step
        bits.append(bit)
        partners.append((lat, other, ex) if axis == "dp" else (other, dp, ex))

    barrier = pltpu.get_barrier_semaphore()
    for dev in partners:
        pl.semaphore_signal(barrier, 1, device_id=dev, device_id_type=pl.DeviceIdType.MESH)
    pl.semaphore_wait(barrier, stages)

    def chunked(count, body):
        chunk = min(count, 1152)
        lax.fori_loop(0, count // chunk, lambda i, c: (body(pl.multiple_of(i * chunk, 16), chunk), c)[1], 0)

    los = []
    lo = jnp.int32(0)
    for k in range(stages):
        half = rows >> (k + 1)
        los.append(lo)
        src = in_ref if k == 0 else sums[k - 1]
        keep = bits[k] * half
        give = (1 - bits[k]) * half

        def narrow(at, chunk, src=src, give=give, k=k):
            staged[k][pl.ds(at, chunk)] = src[pl.ds(pl.multiple_of(give + at, 16), chunk)].astype(jnp.bfloat16)

        chunked(half, narrow)
        copy = pltpu.make_async_remote_copy(
            src_ref=staged[k],
            dst_ref=bufs[k],
            send_sem=rs_send.at[k],
            recv_sem=rs_recv.at[k],
            device_id=partners[k],
            device_id_type=pl.DeviceIdType.MESH,
        )
        copy.start()
        copy.wait()

        def add(at, chunk, src=src, keep=keep, k=k):
            sums[k][pl.ds(at, chunk)] = src[pl.ds(pl.multiple_of(keep + at, 16), chunk)] + bufs[k][
                pl.ds(at, chunk)
            ].astype(jnp.float32)

        chunked(half, add)
        lo = lo + bits[k] * half

    last = rows >> stages
    lo = pl.multiple_of(lo, 16)
    gathered[pl.ds(lo, last)] = sums[stages - 1][...].astype(jnp.bfloat16)
    for k in reversed(range(stages)):
        half = rows >> (k + 1)
        copy = pltpu.make_async_remote_copy(
            src_ref=gathered.at[pl.ds(pl.multiple_of(lo, 16), half)],
            dst_ref=gathered.at[pl.ds(pl.multiple_of(lo, 16), half)],
            send_sem=ag_send.at[k],
            recv_sem=ag_recv.at[k],
            device_id=partners[k],
            device_id_type=pl.DeviceIdType.MESH,
        )
        copy.start()
        copy.wait()
        lo = los[k]

    experts, channels, hidden = out_in.shape
    pieces = hidden // 128
    for e in range(experts):
        for t, dst in enumerate((out_in, out_outt)):
            for c in range(pieces):
                at = ((e * 2 + t) * pieces + c) * channels
                dst[e, :, c * 128:(c + 1) * 128] = gathered[at:at + channels].astype(jnp.float32)


def tree_allreduce(flat, experts, channels, hidden):
    rows = flat.shape[0]
    plan = reduce_plan(lax.axis_size("lat"), lax.axis_size("dp"))
    stages = len(plan)
    scratch = [pltpu.VMEM((rows >> (k + 1), 128), jnp.bfloat16) for k in range(stages)]
    scratch += [pltpu.VMEM((rows >> (k + 1), 128), jnp.float32) for k in range(stages)]
    scratch += [pltpu.VMEM((rows >> (k + 1), 128), jnp.bfloat16) for k in range(stages)]
    scratch += [pltpu.VMEM((rows, 128), jnp.bfloat16)]
    scratch += [pltpu.SemaphoreType.DMA((stages,))] * 4
    return pl.pallas_call(
        lambda *refs: allreduce_kernel(plan, rows, *refs),
        out_shape=[jax.ShapeDtypeStruct((experts, channels, hidden), jnp.float32)] * 2,
        in_specs=[pl.BlockSpec(memory_space=pltpu.VMEM)],
        out_specs=[pl.BlockSpec(memory_space=pltpu.VMEM)] * 2,
        scratch_shapes=scratch,
        compiler_params=pltpu.CompilerParams(
            collective_id=0, has_side_effects=True, vmem_limit_bytes=62 * 1024 * 1024
        ),
    )(flat)

def expert_kernel(x_ref, g_ref, win_ref, wout_ref, out_ref, flat_ref):
    x = x_ref[...]
    g = g_ref[...]
    w_out = wout_ref[...]
    pre = jnp.dot(x, win_ref[...], preferred_element_type=jnp.float32)
    cdf = 0.5 * (1.0 + lax.erf(pre * 0.7071067811865476))
    hidden = (pre * cdf).astype(jnp.bfloat16)
    out_ref[...] = jnp.dot(hidden, w_out, preferred_element_type=jnp.float32).astype(out_ref.dtype)
    grad_out_t = lax.dot_general(g, hidden, (((0,), (0,)), ((), ())), preferred_element_type=jnp.float32)
    back = lax.dot_general(g, w_out, (((1,), (1,)), ((), ())), preferred_element_type=jnp.float32)
    slope = cdf + pre * jnp.exp(-0.5 * pre * pre) * 0.3989422804014327
    scaled = (back * slope).astype(jnp.bfloat16)
    grad_in = lax.dot_general(x, scaled, (((0,), (0,)), ((), ())), preferred_element_type=jnp.float32)
    for c in range(grad_in.shape[1] // 128):
        flat_ref[0, c] = grad_in[:, c * 128:(c + 1) * 128]
        flat_ref[1, c] = grad_out_t[:, c * 128:(c + 1) * 128]


def run_experts(inputs, grads, w_in, w_out):
    experts, tokens, channels = inputs.shape
    hidden = w_in.shape[2]
    pieces = hidden // 128
    tok = pl.BlockSpec((None, tokens, channels), lambda e: (e, 0, 0))
    return pl.pallas_call(
        expert_kernel,
        grid=(experts,),
        out_shape=[
            jax.ShapeDtypeStruct((experts, tokens, channels), jnp.bfloat16),
            jax.ShapeDtypeStruct((experts, 2, pieces, channels, 128), jnp.float32),
        ],
        in_specs=[
            tok,
            tok,
            pl.BlockSpec((None, channels, hidden), lambda e: (e, 0, 0)),
            pl.BlockSpec((None, hidden, channels), lambda e: (e, 0, 0)),
        ],
        out_specs=[tok, pl.BlockSpec((None, 2, pieces, channels, 128), lambda e: (e, 0, 0, 0, 0))],
        compiler_params=pltpu.CompilerParams(vmem_limit_bytes=48 * 1024 * 1024),
    )(inputs, grads, w_in, w_out)


def gelu_slope(values):
    return (
        0.5 * (1.0 + lax.erf(values * 0.7071067811865476))
        + values * jnp.exp(-0.5 * values * values) * 0.3989422804014327
    )


def depthwise(padded, kernel):
    row_count = padded.shape[1] - 6
    col_count = padded.shape[2] - 6
    summed = jnp.zeros((padded.shape[0], row_count, col_count, padded.shape[3]), jnp.float32)
    for row_off in range(7):
        for col_off in range(7):
            window = padded[:, row_off : row_off + row_count, col_off : col_off + col_count, :]
            summed = summed + window.astype(jnp.float32) * kernel[row_off, col_off]
    return summed


def widen(picture):
    return jnp.pad(picture, ((0, 0), (0, 0), (3, 3), (0, 0)))


def dense_block(images, smoothed, ln_gain, w_expand, w_reduce):
    channels = images.shape[-1]
    channel_mean = jnp.mean(smoothed, axis=-1, keepdims=True)
    centered = smoothed - channel_mean
    variance = jnp.mean(centered * centered, axis=-1, keepdims=True)
    normed = (centered * lax.rsqrt(variance + 1e-06) * ln_gain).astype(jnp.bfloat16)
    flat_normed = normed.reshape(-1, channels)
    expanded = jnp.dot(flat_normed, w_expand, preferred_element_type=jnp.float32)
    active = jax.nn.gelu(expanded, approximate=False).astype(jnp.bfloat16)
    reduced = jnp.dot(active, w_reduce, preferred_element_type=jnp.float32)
    dense_out = images.reshape(-1, channels).astype(jnp.float32) + reduced
    return dense_out.astype(jnp.bfloat16).reshape(images.shape)


def expert_pass(inputs, grads_in, w_in, w_out):
    pre_act = jnp.dot(inputs, w_in, preferred_element_type=jnp.float32)
    hidden = jax.nn.gelu(pre_act, approximate=False).astype(jnp.bfloat16)
    outputs = jnp.dot(hidden, w_out, preferred_element_type=jnp.float32).astype(jnp.bfloat16)
    grad_out = jnp.dot(hidden.T, grads_in, preferred_element_type=jnp.float32)
    back_prop = jnp.dot(grads_in, w_out.T, preferred_element_type=jnp.float32)
    scaled = (back_prop * gelu_slope(pre_act)).astype(jnp.bfloat16)
    grad_in = jnp.dot(inputs.T, scaled, preferred_element_type=jnp.float32)
    return (outputs, grad_in, grad_out)


def body(images, cotangent, labels, dw_kernel, ln_gain, w_expand, w_reduce, exp_in, exp_out):
    channels = images.shape[-1]
    padded = with_halo(images, (("lat", 1),), 3)
    smoothed = depthwise(widen(padded), dw_kernel)
    dense_out = dense_block(images, smoothed, ln_gain, w_expand, w_reduce)
    block_width = BLOCK * channels
    blocks = dense_out.reshape(-1, block_width)
    grad_blocks = cotangent.reshape(-1, block_width)
    flat_labels = labels.reshape(-1)
    members = (flat_labels[:, None] == jnp.arange(EXPERTS, dtype=jnp.int32)[None, :]).astype(
        jnp.int32
    )
    before = jnp.sum(jnp.cumsum(members, axis=0) * members, axis=1) - 1
    slot_of = flat_labels * CAP + before
    placer = (jnp.arange(EXPERTS * CAP, dtype=jnp.int32)[:, None] == slot_of[None, :]).astype(
        jnp.bfloat16
    )
    outgoing = (
        jnp.dot(placer, blocks, preferred_element_type=jnp.float32)
        .astype(jnp.bfloat16)
        .reshape(EXPERTS, CAP, block_width)
    )
    outgoing_grads = (
        jnp.dot(placer, grad_blocks, preferred_element_type=jnp.float32)
        .astype(jnp.bfloat16)
        .reshape(EXPERTS, CAP, block_width)
    )

    arrived, arrived_grads = (
        lax.all_to_all(outgoing, "exp", split_axis=0, concat_axis=1, tiled=True),
        lax.all_to_all(outgoing_grads, "exp", split_axis=0, concat_axis=1, tiled=True),
    )
    local = arrived.shape[0]
    results, flat = run_experts(
        arrived.reshape(local, -1, channels), arrived_grads.reshape(local, -1, channels), exp_in, exp_out
    )
    returned = lax.all_to_all(results.reshape(arrived.shape), "exp", split_axis=1, concat_axis=0, tiled=True)
    grad_in, grad_out_t = tree_allreduce(flat.reshape(-1, 128), local, channels, exp_in.shape[2])
    grad_out = jnp.transpose(grad_out_t, (0, 2, 1))
    expert_out = jnp.dot(
        placer.T, returned.reshape(EXPERTS * CAP, block_width), preferred_element_type=jnp.float32
    ).astype(jnp.bfloat16)
    output = (
        dense_out.astype(jnp.float32) + expert_out.reshape(dense_out.shape).astype(jnp.float32)
    ).astype(jnp.bfloat16)
    return (output, grad_in, grad_out)


def solution(mesh):
    in_specs = (
        P(("dp", "exp"), "lat", None, None),
        P(("dp", "exp"), "lat", None, None),
        P(("dp", "exp"), "lat", None, None),
        P(),
        P(),
        P(),
        P(),
        P("exp", None, None),
        P("exp", None, None),
    )
    out_specs = (P(("dp", "exp"), "lat", None, None), P("exp", None, None), P("exp", None, None))
    return jax.shard_map(body, mesh=mesh, in_specs=in_specs, out_specs=out_specs, check_vma=False)
```

```python
import jax
import jax.numpy as jnp
from jax import lax
from jax.sharding import PartitionSpec as P
from jax.experimental import pallas as pl
from jax.experimental.pallas import tpu as pltpu

EXPERTS = 16
BLOCK = 128
CAP = 3


def with_halo(block, sides, width):
    for axis, dim in sides:
        count = lax.axis_size(axis)
        forward = [(i, i + 1) for i in range(count - 1)]
        backward = [(target, source) for source, target in forward]
        low = lax.ppermute(
            lax.slice_in_dim(block, block.shape[dim] - width, None, axis=dim), axis, forward
        )
        high = lax.ppermute(lax.slice_in_dim(block, 0, width, axis=dim), axis, backward)
        block = jnp.concatenate([low, block, high], axis=dim)
    return block


def reduce_plan(lat_size, dp_size):
    dp_bits = dp_size.bit_length() - 1
    rest = list(range(1, dp_bits))
    other = rest[2:] + rest[:2] if len(rest) > 2 else rest
    plan = [("dp", 0, 0)] + [("dp", a, b) for a, b in zip(rest, other)]
    plan += [("lat", 0, 0)] * (lat_size.bit_length() - 1)
    return plan


def allreduce_kernel(plan, rows, in_ref, out_in, out_outt, *scratch):
    stages = len(plan)
    bufs = scratch[:stages]
    sums = scratch[stages:2 * stages]
    staged = scratch[2 * stages:3 * stages]
    gathered = scratch[3 * stages]
    rs_send, rs_recv, ag_send, ag_recv = scratch[3 * stages + 1:]
    lat = lax.axis_index("lat")
    dp = lax.axis_index("dp")
    ex = lax.axis_index("exp")
    core = dp % 2

    bits, partners = [], []
    for axis, b0, b1 in plan:
        me = dp if axis == "dp" else lat
        bit = jnp.where(core == 0, (me // (1 << b0)) % 2, (me // (1 << b1)) % 2)
        step = jnp.where(core == 0, 1 << b0, 1 << b1)
        other = me + (1 - 2 * bit) * step
        bits.append(bit)
        partners.append((lat, other, ex) if axis == "dp" else (other, dp, ex))

    barrier = pltpu.get_barrier_semaphore()
    for dev in partners:
        pl.semaphore_signal(barrier, 1, device_id=dev, device_id_type=pl.DeviceIdType.MESH)
    pl.semaphore_wait(barrier, stages)

    def chunked(count, body):
        chunk = min(count, 1152)
        lax.fori_loop(0, count // chunk, lambda i, c: (body(pl.multiple_of(i * chunk, 16), chunk), c)[1], 0)

    los = []
    lo = jnp.int32(0)
    for k in range(stages):
        half = rows >> (k + 1)
        los.append(lo)
        src = in_ref if k == 0 else sums[k - 1]
        keep = bits[k] * half
        give = (1 - bits[k]) * half

        def narrow(at, chunk, src=src, give=give, k=k):
            staged[k][pl.ds(at, chunk)] = src[pl.ds(pl.multiple_of(give + at, 16), chunk)].astype(jnp.bfloat16)

        chunked(half, narrow)
        copy = pltpu.make_async_remote_copy(
            src_ref=staged[k],
            dst_ref=bufs[k],
            send_sem=rs_send.at[k],
            recv_sem=rs_recv.at[k],
            device_id=partners[k],
            device_id_type=pl.DeviceIdType.MESH,
        )
        copy.start()
        copy.wait()

        def add(at, chunk, src=src, keep=keep, k=k):
            sums[k][pl.ds(at, chunk)] = src[pl.ds(pl.multiple_of(keep + at, 16), chunk)] + bufs[k][
                pl.ds(at, chunk)
            ].astype(jnp.float32)

        chunked(half, add)
        lo = lo + bits[k] * half

    last = rows >> stages
    lo = pl.multiple_of(lo, 16)
    gathered[pl.ds(lo, last)] = sums[stages - 1][...].astype(jnp.bfloat16)
    for k in reversed(range(stages)):
        half = rows >> (k + 1)
        copy = pltpu.make_async_remote_copy(
            src_ref=gathered.at[pl.ds(pl.multiple_of(lo, 16), half)],
            dst_ref=gathered.at[pl.ds(pl.multiple_of(lo, 16), half)],
            send_sem=ag_send.at[k],
            recv_sem=ag_recv.at[k],
            device_id=partners[k],
            device_id_type=pl.DeviceIdType.MESH,
        )
        copy.start()
        copy.wait()
        lo = los[k]

    experts, channels, hidden = out_in.shape
    pieces = hidden // 128
    for e in range(experts):
        for t, dst in enumerate((out_in, out_outt)):
            for c in range(pieces):
                at = ((e * 2 + t) * pieces + c) * channels
                dst[e, :, c * 128:(c + 1) * 128] = gathered[at:at + channels].astype(jnp.float32)


def tree_allreduce(flat, experts, channels, hidden):
    rows = flat.shape[0]
    plan = reduce_plan(lax.axis_size("lat"), lax.axis_size("dp"))
    stages = len(plan)
    scratch = [pltpu.VMEM((rows >> (k + 1), 128), jnp.bfloat16) for k in range(stages)]
    scratch += [pltpu.VMEM((rows >> (k + 1), 128), jnp.float32) for k in range(stages)]
    scratch += [pltpu.VMEM((rows >> (k + 1), 128), jnp.bfloat16) for k in range(stages)]
    scratch += [pltpu.VMEM((rows, 128), jnp.bfloat16)]
    scratch += [pltpu.SemaphoreType.DMA((stages,))] * 4
    return pl.pallas_call(
        lambda *refs: allreduce_kernel(plan, rows, *refs),
        out_shape=[jax.ShapeDtypeStruct((experts, channels, hidden), jnp.float32)] * 2,
        in_specs=[pl.BlockSpec(memory_space=pltpu.VMEM)],
        out_specs=[pl.BlockSpec(memory_space=pltpu.VMEM)] * 2,
        scratch_shapes=scratch,
        compiler_params=pltpu.CompilerParams(
            collective_id=0, has_side_effects=True, vmem_limit_bytes=62 * 1024 * 1024
        ),
    )(flat)

def expert_kernel(x_ref, g_ref, win_ref, wout_ref, out_ref, flat_ref):
    x = x_ref[...]
    g = g_ref[...]
    w_out = wout_ref[...]
    pre = jnp.dot(x, win_ref[...], preferred_element_type=jnp.float32)
    cdf = 0.5 * (1.0 + lax.erf(pre * 0.7071067811865476))
    hidden = (pre * cdf).astype(jnp.bfloat16)
    out_ref[...] = jnp.dot(hidden, w_out, preferred_element_type=jnp.float32).astype(out_ref.dtype)
    grad_out_t = lax.dot_general(g, hidden, (((0,), (0,)), ((), ())), preferred_element_type=jnp.float32)
    back = lax.dot_general(g, w_out, (((1,), (1,)), ((), ())), preferred_element_type=jnp.float32)
    slope = cdf + pre * jnp.exp(-0.5 * pre * pre) * 0.3989422804014327
    scaled = (back * slope).astype(jnp.bfloat16)
    grad_in = lax.dot_general(x, scaled, (((0,), (0,)), ((), ())), preferred_element_type=jnp.float32)
    for c in range(grad_in.shape[1] // 128):
        flat_ref[0, c] = grad_in[:, c * 128:(c + 1) * 128]
        flat_ref[1, c] = grad_out_t[:, c * 128:(c + 1) * 128]


def run_experts(inputs, grads, w_in, w_out):
    experts, tokens, channels = inputs.shape
    hidden = w_in.shape[2]
    pieces = hidden // 128
    tok = pl.BlockSpec((None, tokens, channels), lambda e: (e, 0, 0))
    return pl.pallas_call(
        expert_kernel,
        grid=(experts,),
        out_shape=[
            jax.ShapeDtypeStruct((experts, tokens, channels), jnp.bfloat16),
            jax.ShapeDtypeStruct((experts, 2, pieces, channels, 128), jnp.float32),
        ],
        in_specs=[
            tok,
            tok,
            pl.BlockSpec((None, channels, hidden), lambda e: (e, 0, 0)),
            pl.BlockSpec((None, hidden, channels), lambda e: (e, 0, 0)),
        ],
        out_specs=[tok, pl.BlockSpec((None, 2, pieces, channels, 128), lambda e: (e, 0, 0, 0, 0))],
        compiler_params=pltpu.CompilerParams(vmem_limit_bytes=48 * 1024 * 1024),
    )(inputs, grads, w_in, w_out)


def gelu_slope(values):
    return (
        0.5 * (1.0 + lax.erf(values * 0.7071067811865476))
        + values * jnp.exp(-0.5 * values * values) * 0.3989422804014327
    )


def depthwise(padded, kernel):
    row_count = padded.shape[1] - 6
    col_count = padded.shape[2] - 6
    summed = jnp.zeros((padded.shape[0], row_count, col_count, padded.shape[3]), jnp.float32)
    for row_off in range(7):
        for col_off in range(7):
            window = padded[:, row_off : row_off + row_count, col_off : col_off + col_count, :]
            summed = summed + window.astype(jnp.float32) * kernel[row_off, col_off]
    return summed


def widen(picture):
    return jnp.pad(picture, ((0, 0), (0, 0), (3, 3), (0, 0)))


def dense_block(images, smoothed, ln_gain, w_expand, w_reduce):
    channels = images.shape[-1]
    channel_mean = jnp.mean(smoothed, axis=-1, keepdims=True)
    centered = smoothed - channel_mean
    variance = jnp.mean(centered * centered, axis=-1, keepdims=True)
    normed = (centered * lax.rsqrt(variance + 1e-06) * ln_gain).astype(jnp.bfloat16)
    flat_normed = normed.reshape(-1, channels)
    expanded = jnp.dot(flat_normed, w_expand, preferred_element_type=jnp.float32)
    active = jax.nn.gelu(expanded, approximate=False).astype(jnp.bfloat16)
    reduced = jnp.dot(active, w_reduce, preferred_element_type=jnp.float32)
    dense_out = images.reshape(-1, channels).astype(jnp.float32) + reduced
    return dense_out.astype(jnp.bfloat16).reshape(images.shape)


def expert_pass(inputs, grads_in, w_in, w_out):
    pre_act = jnp.dot(inputs, w_in, preferred_element_type=jnp.float32)
    hidden = jax.nn.gelu(pre_act, approximate=False).astype(jnp.bfloat16)
    outputs = jnp.dot(hidden, w_out, preferred_element_type=jnp.float32).astype(jnp.bfloat16)
    grad_out = jnp.dot(hidden.T, grads_in, preferred_element_type=jnp.float32)
    back_prop = jnp.dot(grads_in, w_out.T, preferred_element_type=jnp.float32)
    scaled = (back_prop * gelu_slope(pre_act)).astype(jnp.bfloat16)
    grad_in = jnp.dot(inputs.T, scaled, preferred_element_type=jnp.float32)
    return (outputs, grad_in, grad_out)


def body(images, cotangent, labels, dw_kernel, ln_gain, w_expand, w_reduce, exp_in, exp_out):
    channels = images.shape[-1]
    padded = with_halo(images, (("lat", 1),), 3)
    smoothed = depthwise(widen(padded), dw_kernel)
    dense_out = dense_block(images, smoothed, ln_gain, w_expand, w_reduce)
    blocks = dense_out.reshape(-1, BLOCK, channels)
    grad_blocks = cotangent.reshape(-1, BLOCK, channels)
    flat_labels = labels.reshape(-1)
    members = (flat_labels[:, None] == jnp.arange(EXPERTS, dtype=jnp.int32)[None, :]).astype(
        jnp.int32
    )
    before = jnp.sum(jnp.cumsum(members, axis=0) * members, axis=1) - 1
    slot_of = flat_labels * CAP + before
    placer = jnp.arange(EXPERTS * CAP, dtype=jnp.int32)[:, None] == slot_of[None, :]
    block_of_slot = jnp.argmax(placer, axis=1)
    filled = jnp.any(placer, axis=1)[:, None, None]
    outgoing = blocks[block_of_slot].reshape(EXPERTS, CAP, BLOCK, channels)
    outgoing_grads = jnp.where(filled, grad_blocks[block_of_slot], jnp.zeros((), jnp.bfloat16)).reshape(
        EXPERTS, CAP, BLOCK, channels
    )
    arrived, arrived_grads = (
        lax.all_to_all(outgoing, "exp", split_axis=0, concat_axis=1, tiled=True),
        lax.all_to_all(outgoing_grads, "exp", split_axis=0, concat_axis=1, tiled=True),
    )
    local = arrived.shape[0]
    results, flat = run_experts(
        arrived.reshape(local, -1, channels), arrived_grads.reshape(local, -1, channels), exp_in, exp_out
    )
    returned = lax.all_to_all(results.reshape(arrived.shape), "exp", split_axis=1, concat_axis=0, tiled=True)
    grad_in, grad_out_t = tree_allreduce(flat.reshape(-1, 128), local, channels, exp_in.shape[2])
    grad_out = jnp.transpose(grad_out_t, (0, 2, 1))
    expert_out = returned.reshape(EXPERTS * CAP, BLOCK, channels)[slot_of]
    output = (
        dense_out.astype(jnp.float32) + expert_out.reshape(dense_out.shape).astype(jnp.float32)
    ).astype(jnp.bfloat16)
    return (output, grad_in, grad_out)


def solution(mesh):
    in_specs = (
        P(("dp", "exp"), "lat", None, None),
        P(("dp", "exp"), "lat", None, None),
        P(("dp", "exp"), "lat", None, None),
        P(),
        P(),
        P(),
        P(),
        P("exp", None, None),
        P("exp", None, None),
    )
    out_specs = (P(("dp", "exp"), "lat", None, None), P("exp", None, None), P("exp", None, None))
    return jax.shard_map(body, mesh=mesh, in_specs=in_specs, out_specs=out_specs, check_vma=False)
```

```python
import jax
import jax.numpy as jnp
from jax import lax
from jax.sharding import PartitionSpec as P
from jax.experimental import pallas as pl
from jax.experimental.pallas import tpu as pltpu

EXPERTS = 16
BLOCK = 128
CAP = 3


def with_halo(block, sides, width):
    for axis, dim in sides:
        count = lax.axis_size(axis)
        forward = [(i, i + 1) for i in range(count - 1)]
        backward = [(target, source) for source, target in forward]
        low = lax.ppermute(
            lax.slice_in_dim(block, block.shape[dim] - width, None, axis=dim), axis, forward
        )
        high = lax.ppermute(lax.slice_in_dim(block, 0, width, axis=dim), axis, backward)
        block = jnp.concatenate([low, block, high], axis=dim)
    return block


def reduce_plan(lat_size, dp_size):
    dp_bits = dp_size.bit_length() - 1
    rest = list(range(1, dp_bits))
    other = rest[2:] + rest[:2] if len(rest) > 2 else rest
    plan = [("dp", 0, 0)] + [("dp", a, b) for a, b in zip(rest, other)]
    plan += [("lat", 0, 0)] * (lat_size.bit_length() - 1)
    return plan


def allreduce_kernel(plan, rows, in_ref, out_in, out_outt, *scratch):
    stages = len(plan)
    bufs = scratch[:stages]
    sums = scratch[stages:2 * stages]
    staged = scratch[2 * stages:3 * stages]
    gathered = scratch[3 * stages]
    rs_send, rs_recv, ag_send, ag_recv = scratch[3 * stages + 1:]
    lat = lax.axis_index("lat")
    dp = lax.axis_index("dp")
    ex = lax.axis_index("exp")
    core = dp % 2

    bits, partners = [], []
    for axis, b0, b1 in plan:
        me = dp if axis == "dp" else lat
        bit = jnp.where(core == 0, (me // (1 << b0)) % 2, (me // (1 << b1)) % 2)
        step = jnp.where(core == 0, 1 << b0, 1 << b1)
        other = me + (1 - 2 * bit) * step
        bits.append(bit)
        partners.append((lat, other, ex) if axis == "dp" else (other, dp, ex))

    barrier = pltpu.get_barrier_semaphore()
    for dev in partners:
        pl.semaphore_signal(barrier, 1, device_id=dev, device_id_type=pl.DeviceIdType.MESH)
    pl.semaphore_wait(barrier, stages)

    def chunked(count, body):
        chunk = min(count, 1152)
        lax.fori_loop(0, count // chunk, lambda i, c: (body(pl.multiple_of(i * chunk, 16), chunk), c)[1], 0)

    los = []
    lo = jnp.int32(0)
    for k in range(stages):
        half = rows >> (k + 1)
        los.append(lo)
        src = in_ref if k == 0 else sums[k - 1]
        keep = bits[k] * half
        give = (1 - bits[k]) * half

        def narrow(at, chunk, src=src, give=give, k=k):
            staged[k][pl.ds(at, chunk)] = src[pl.ds(pl.multiple_of(give + at, 16), chunk)].astype(jnp.bfloat16)

        chunked(half, narrow)
        copy = pltpu.make_async_remote_copy(
            src_ref=staged[k],
            dst_ref=bufs[k],
            send_sem=rs_send.at[k],
            recv_sem=rs_recv.at[k],
            device_id=partners[k],
            device_id_type=pl.DeviceIdType.MESH,
        )
        copy.start()
        copy.wait()

        def add(at, chunk, src=src, keep=keep, k=k):
            sums[k][pl.ds(at, chunk)] = src[pl.ds(pl.multiple_of(keep + at, 16), chunk)] + bufs[k][
                pl.ds(at, chunk)
            ].astype(jnp.float32)

        chunked(half, add)
        lo = lo + bits[k] * half

    last = rows >> stages
    lo = pl.multiple_of(lo, 16)
    gathered[pl.ds(lo, last)] = sums[stages - 1][...].astype(jnp.bfloat16)
    for k in reversed(range(stages)):
        half = rows >> (k + 1)
        copy = pltpu.make_async_remote_copy(
            src_ref=gathered.at[pl.ds(pl.multiple_of(lo, 16), half)],
            dst_ref=gathered.at[pl.ds(pl.multiple_of(lo, 16), half)],
            send_sem=ag_send.at[k],
            recv_sem=ag_recv.at[k],
            device_id=partners[k],
            device_id_type=pl.DeviceIdType.MESH,
        )
        copy.start()
        copy.wait()
        lo = los[k]

    experts, channels, hidden = out_in.shape
    pieces = hidden // 128
    for e in range(experts):
        for t, dst in enumerate((out_in, out_outt)):
            for c in range(pieces):
                at = ((e * 2 + t) * pieces + c) * channels
                dst[e, :, c * 128:(c + 1) * 128] = gathered[at:at + channels].astype(jnp.float32)


def tree_allreduce(flat, experts, channels, hidden):
    rows = flat.shape[0]
    plan = reduce_plan(lax.axis_size("lat"), lax.axis_size("dp"))
    stages = len(plan)
    scratch = [pltpu.VMEM((rows >> (k + 1), 128), jnp.bfloat16) for k in range(stages)]
    scratch += [pltpu.VMEM((rows >> (k + 1), 128), jnp.float32) for k in range(stages)]
    scratch += [pltpu.VMEM((rows >> (k + 1), 128), jnp.bfloat16) for k in range(stages)]
    scratch += [pltpu.VMEM((rows, 128), jnp.bfloat16)]
    scratch += [pltpu.SemaphoreType.DMA((stages,))] * 4
    return pl.pallas_call(
        lambda *refs: allreduce_kernel(plan, rows, *refs),
        out_shape=[jax.ShapeDtypeStruct((experts, channels, hidden), jnp.float32)] * 2,
        in_specs=[pl.BlockSpec(memory_space=pltpu.VMEM)],
        out_specs=[pl.BlockSpec(memory_space=pltpu.VMEM)] * 2,
        scratch_shapes=scratch,
        compiler_params=pltpu.CompilerParams(
            collective_id=0, has_side_effects=True, vmem_limit_bytes=62 * 1024 * 1024
        ),
    )(flat)

def expert_kernel(x_ref, g_ref, win_ref, wout_ref, out_ref, flat_ref):
    slots = x_ref.shape[0]
    x_t = jnp.concatenate([x_ref[s] for s in range(slots)], axis=1)
    g_t = jnp.concatenate([g_ref[s] for s in range(slots)], axis=1)
    w_out_t = wout_ref[...]
    pre = lax.dot_general(x_t, win_ref[...], (((0,), (0,)), ((), ())), preferred_element_type=jnp.float32)
    cdf = 0.5 * (1.0 + lax.erf(pre * 0.7071067811865476))
    hidden = (pre * cdf).astype(jnp.bfloat16)
    out_t = lax.dot_general(w_out_t, hidden, (((1,), (1,)), ((), ())), preferred_element_type=jnp.float32)
    out_t = out_t.astype(out_ref.dtype)
    width = out_ref.shape[2]
    for s in range(slots):
        out_ref[s] = out_t[:, s * width:(s + 1) * width]
    grad_out_t = jnp.dot(g_t, hidden, preferred_element_type=jnp.float32)
    back = lax.dot_general(g_t, w_out_t, (((0,), (0,)), ((), ())), preferred_element_type=jnp.float32)
    slope = cdf + pre * jnp.exp(-0.5 * pre * pre) * 0.3989422804014327
    scaled = (back * slope).astype(jnp.bfloat16)
    grad_in = jnp.dot(x_t, scaled, preferred_element_type=jnp.float32)
    for c in range(grad_in.shape[1] // 128):
        flat_ref[0, c] = grad_in[:, c * 128:(c + 1) * 128]
        flat_ref[1, c] = grad_out_t[:, c * 128:(c + 1) * 128]


def run_experts(inputs, grads, w_in, w_out_t):
    experts, slots, channels, width = inputs.shape
    hidden = w_in.shape[2]
    pieces = hidden // 128
    tok = pl.BlockSpec((None, slots, channels, width), lambda e: (e, 0, 0, 0))
    weight = pl.BlockSpec((None, channels, hidden), lambda e: (e, 0, 0))
    return pl.pallas_call(
        expert_kernel,
        grid=(experts,),
        out_shape=[
            jax.ShapeDtypeStruct(inputs.shape, jnp.bfloat16),
            jax.ShapeDtypeStruct((experts, 2, pieces, channels, 128), jnp.float32),
        ],
        in_specs=[tok, tok, weight, weight],
        out_specs=[tok, pl.BlockSpec((None, 2, pieces, channels, 128), lambda e: (e, 0, 0, 0, 0))],
        compiler_params=pltpu.CompilerParams(vmem_limit_bytes=48 * 1024 * 1024),
    )(inputs, grads, w_in, w_out_t)

def gelu_slope(values):
    return (
        0.5 * (1.0 + lax.erf(values * 0.7071067811865476))
        + values * jnp.exp(-0.5 * values * values) * 0.3989422804014327
    )


def depthwise(padded, kernel):
    row_count = padded.shape[1] - 6
    col_count = padded.shape[2] - 6
    summed = jnp.zeros((padded.shape[0], row_count, col_count, padded.shape[3]), jnp.float32)
    for row_off in range(7):
        for col_off in range(7):
            window = padded[:, row_off : row_off + row_count, col_off : col_off + col_count, :]
            summed = summed + window.astype(jnp.float32) * kernel[row_off, col_off]
    return summed


def widen(picture):
    return jnp.pad(picture, ((0, 0), (0, 0), (3, 3), (0, 0)))


def dense_block(images, smoothed, ln_gain, w_expand, w_reduce):
    channels = images.shape[-1]
    channel_mean = jnp.mean(smoothed, axis=-1, keepdims=True)
    centered = smoothed - channel_mean
    variance = jnp.mean(centered * centered, axis=-1, keepdims=True)
    normed = (centered * lax.rsqrt(variance + 1e-06) * ln_gain).astype(jnp.bfloat16)
    flat_normed = normed.reshape(-1, channels)
    expanded = jnp.dot(flat_normed, w_expand, preferred_element_type=jnp.float32)
    active = jax.nn.gelu(expanded, approximate=False).astype(jnp.bfloat16)
    reduced = jnp.dot(active, w_reduce, preferred_element_type=jnp.float32)
    dense_out = images.reshape(-1, channels).astype(jnp.float32) + reduced
    return dense_out.astype(jnp.bfloat16).reshape(images.shape)


def expert_pass(inputs, grads_in, w_in, w_out):
    pre_act = jnp.dot(inputs, w_in, preferred_element_type=jnp.float32)
    hidden = jax.nn.gelu(pre_act, approximate=False).astype(jnp.bfloat16)
    outputs = jnp.dot(hidden, w_out, preferred_element_type=jnp.float32).astype(jnp.bfloat16)
    grad_out = jnp.dot(hidden.T, grads_in, preferred_element_type=jnp.float32)
    back_prop = jnp.dot(grads_in, w_out.T, preferred_element_type=jnp.float32)
    scaled = (back_prop * gelu_slope(pre_act)).astype(jnp.bfloat16)
    grad_in = jnp.dot(inputs.T, scaled, preferred_element_type=jnp.float32)
    return (outputs, grad_in, grad_out)


def body(images, cotangent, labels, dw_kernel, ln_gain, w_expand, w_reduce, exp_in, exp_out):
    channels = images.shape[-1]
    padded = with_halo(images, (("lat", 1),), 3)
    smoothed = depthwise(widen(padded), dw_kernel)
    dense_out = dense_block(images, smoothed, ln_gain, w_expand, w_reduce)
    rows, width = images.shape[1], images.shape[2]
    per_row = width // BLOCK

    def to_blocks(pixels):
        pixels = pixels.reshape(rows, per_row, BLOCK, channels)
        return jnp.transpose(pixels, (0, 1, 3, 2)).reshape(rows * per_row, channels, BLOCK)

    blocks = to_blocks(dense_out)
    grad_blocks = to_blocks(cotangent)
    flat_labels = labels.reshape(-1)
    members = (flat_labels[:, None] == jnp.arange(EXPERTS, dtype=jnp.int32)[None, :]).astype(
        jnp.int32
    )
    before = jnp.sum(jnp.cumsum(members, axis=0) * members, axis=1) - 1
    slot_of = flat_labels * CAP + before
    placer = jnp.arange(EXPERTS * CAP, dtype=jnp.int32)[:, None] == slot_of[None, :]
    block_of_slot = jnp.argmax(placer, axis=1)
    filled = jnp.any(placer, axis=1)[:, None, None]
    outgoing = blocks[block_of_slot].reshape(EXPERTS, CAP, channels, BLOCK)
    outgoing_grads = jnp.where(filled, grad_blocks[block_of_slot], jnp.zeros((), jnp.bfloat16)).reshape(
        EXPERTS, CAP, channels, BLOCK
    )
    arrived, arrived_grads = (
        lax.all_to_all(outgoing, "exp", split_axis=0, concat_axis=1, tiled=True),
        lax.all_to_all(outgoing_grads, "exp", split_axis=0, concat_axis=1, tiled=True),
    )
    local = arrived.shape[0]
    results, flat = run_experts(arrived, arrived_grads, exp_in, jnp.transpose(exp_out, (0, 2, 1)))
    returned = lax.all_to_all(results, "exp", split_axis=1, concat_axis=0, tiled=True)
    grad_in, grad_out_t = tree_allreduce(flat.reshape(-1, 128), local, channels, exp_in.shape[2])
    grad_out = jnp.transpose(grad_out_t, (0, 2, 1))
    expert_blocks = returned.reshape(EXPERTS * CAP, channels, BLOCK)[slot_of]
    expert_out = jnp.transpose(expert_blocks.reshape(rows, per_row, channels, BLOCK), (0, 1, 3, 2))
    output = (
        dense_out.astype(jnp.float32) + expert_out.reshape(dense_out.shape).astype(jnp.float32)
    ).astype(jnp.bfloat16)
    return (output, grad_in, grad_out)


def solution(mesh):
    in_specs = (
        P(("dp", "exp"), "lat", None, None),
        P(("dp", "exp"), "lat", None, None),
        P(("dp", "exp"), "lat", None, None),
        P(),
        P(),
        P(),
        P(),
        P("exp", None, None),
        P("exp", None, None),
    )
    out_specs = (P(("dp", "exp"), "lat", None, None), P("exp", None, None), P("exp", None, None))
    return jax.shard_map(body, mesh=mesh, in_specs=in_specs, out_specs=out_specs, check_vma=False)
```

```python
import jax
import jax.numpy as jnp
from jax import lax
from jax.sharding import PartitionSpec as P
from jax.experimental import pallas as pl
from jax.experimental.pallas import tpu as pltpu

EXPERTS = 16
BLOCK = 128
CAP = 3


def with_halo(block, sides, width):
    for axis, dim in sides:
        count = lax.axis_size(axis)
        forward = [(i, i + 1) for i in range(count - 1)]
        backward = [(target, source) for source, target in forward]
        low = lax.ppermute(
            lax.slice_in_dim(block, block.shape[dim] - width, None, axis=dim), axis, forward
        )
        high = lax.ppermute(lax.slice_in_dim(block, 0, width, axis=dim), axis, backward)
        block = jnp.concatenate([low, block, high], axis=dim)
    return block


def reduce_plan(lat_size, dp_size):
    dp_bits = dp_size.bit_length() - 1
    rest = list(range(1, dp_bits))
    other = rest[2:] + rest[:2] if len(rest) > 2 else rest
    plan = [("dp", 0, 0)] + [("dp", a, b) for a, b in zip(rest, other)]
    plan += [("lat", 0, 0)] * (lat_size.bit_length() - 1)
    return plan


def plan_bits(plan):
    lat = lax.axis_index("lat")
    dp = lax.axis_index("dp")
    ex = lax.axis_index("exp")
    core = dp % 2
    bits, partners = [], []
    for axis, b0, b1 in plan:
        me = dp if axis == "dp" else lat
        bit = jnp.where(core == 0, (me // (1 << b0)) % 2, (me // (1 << b1)) % 2)
        step = jnp.where(core == 0, 1 << b0, 1 << b1)
        other = me + (1 - 2 * bit) * step
        bits.append(bit)
        partners.append((lat, other, ex) if axis == "dp" else (other, dp, ex))
    barrier = pltpu.get_barrier_semaphore()
    for dev in partners:
        pl.semaphore_signal(barrier, 1, device_id=dev, device_id_type=pl.DeviceIdType.MESH)
    pl.semaphore_wait(barrier, len(plan))
    return bits, partners


def chunked(count, body):
    chunk = min(count, 1152)
    lax.fori_loop(0, count // chunk, lambda i, c: (body(pl.multiple_of(i * chunk, 16), chunk), c)[1], 0)


def scatter_kernel(plan, rows, in_ref, seg_ref, *scratch):
    stages = len(plan)
    bufs = scratch[:stages]
    sums = scratch[stages:2 * stages]
    staged = scratch[2 * stages:3 * stages]
    rs_send, rs_recv = scratch[3 * stages:]
    bits, partners = plan_bits(plan)
    for k in range(stages):
        half = rows >> (k + 1)
        src = in_ref if k == 0 else sums[k - 1]
        keep = bits[k] * half
        give = (1 - bits[k]) * half

        def narrow(at, chunk, src=src, give=give, k=k):
            staged[k][pl.ds(at, chunk)] = src[pl.ds(pl.multiple_of(give + at, 16), chunk)].astype(jnp.bfloat16)

        chunked(half, narrow)
        copy = pltpu.make_async_remote_copy(
            src_ref=staged[k],
            dst_ref=bufs[k],
            send_sem=rs_send.at[k],
            recv_sem=rs_recv.at[k],
            device_id=partners[k],
            device_id_type=pl.DeviceIdType.MESH,
        )
        copy.start()
        copy.wait()

        def add(at, chunk, src=src, keep=keep, k=k):
            sums[k][pl.ds(at, chunk)] = src[pl.ds(pl.multiple_of(keep + at, 16), chunk)] + bufs[k][
                pl.ds(at, chunk)
            ].astype(jnp.float32)

        chunked(half, add)
    seg_ref[...] = sums[stages - 1][...]


def gather_kernel(plan, rows, seg_ref, after_ref, out_in, out_outt, gathered, ag_send, ag_recv):
    stages = len(plan)
    bits, partners = plan_bits(plan)
    los = [jnp.int32(0)]
    for k in range(stages):
        los.append(los[-1] + bits[k] * (rows >> (k + 1)))
    lo = pl.multiple_of(los[stages], 16)
    gathered[pl.ds(lo, rows >> stages)] = seg_ref[...].astype(jnp.bfloat16)
    for k in reversed(range(stages)):
        half = rows >> (k + 1)
        at = pl.multiple_of(los[k + 1], 16)
        copy = pltpu.make_async_remote_copy(
            src_ref=gathered.at[pl.ds(at, half)],
            dst_ref=gathered.at[pl.ds(at, half)],
            send_sem=ag_send.at[k],
            recv_sem=ag_recv.at[k],
            device_id=partners[k],
            device_id_type=pl.DeviceIdType.MESH,
        )
        copy.start()
        copy.wait()
    experts, channels, hidden = out_in.shape
    pieces = hidden // 128
    for e in range(experts):
        for t, dst in enumerate((out_in, out_outt)):
            for c in range(pieces):
                at = ((e * 2 + t) * pieces + c) * channels
                dst[e, :, c * 128:(c + 1) * 128] = gathered[at:at + channels].astype(jnp.float32)


def reduce_scatter(flat):
    rows = flat.shape[0]
    plan = reduce_plan(lax.axis_size("lat"), lax.axis_size("dp"))
    stages = len(plan)
    scratch = [pltpu.VMEM((rows >> (k + 1), 128), jnp.bfloat16) for k in range(stages)]
    scratch += [pltpu.VMEM((rows >> (k + 1), 128), jnp.float32) for k in range(stages)]
    scratch += [pltpu.VMEM((rows >> (k + 1), 128), jnp.bfloat16) for k in range(stages)]
    scratch += [pltpu.SemaphoreType.DMA((stages,))] * 2
    return pl.pallas_call(
        lambda *refs: scatter_kernel(plan, rows, *refs),
        out_shape=jax.ShapeDtypeStruct((rows >> stages, 128), jnp.float32),
        in_specs=[pl.BlockSpec(memory_space=pltpu.VMEM)],
        out_specs=pl.BlockSpec(memory_space=pltpu.VMEM),
        scratch_shapes=scratch,
        compiler_params=pltpu.CompilerParams(
            collective_id=0, has_side_effects=True, vmem_limit_bytes=62 * 1024 * 1024
        ),
    )(flat)


def all_gather(seg, after, rows, experts, channels, hidden):
    plan = reduce_plan(lax.axis_size("lat"), lax.axis_size("dp"))
    stages = len(plan)
    return pl.pallas_call(
        lambda *refs: gather_kernel(plan, rows, *refs),
        out_shape=[jax.ShapeDtypeStruct((experts, channels, hidden), jnp.float32)] * 2,
        in_specs=[pl.BlockSpec(memory_space=pltpu.VMEM), pl.BlockSpec(memory_space=pl.ANY)],
        out_specs=[pl.BlockSpec(memory_space=pltpu.VMEM)] * 2,
        scratch_shapes=[pltpu.VMEM((rows, 128), jnp.bfloat16)] + [pltpu.SemaphoreType.DMA((stages,))] * 2,
        compiler_params=pltpu.CompilerParams(
            collective_id=1, has_side_effects=True, vmem_limit_bytes=62 * 1024 * 1024
        ),
    )(seg, after)

def expert_kernel(x_ref, g_ref, win_ref, wout_ref, out_ref, flat_ref):
    slots = x_ref.shape[0]
    x_t = jnp.concatenate([x_ref[s] for s in range(slots)], axis=1)
    g_t = jnp.concatenate([g_ref[s] for s in range(slots)], axis=1)
    w_out_t = wout_ref[...]
    pre = lax.dot_general(x_t, win_ref[...], (((0,), (0,)), ((), ())), preferred_element_type=jnp.float32)
    cdf = 0.5 * (1.0 + lax.erf(pre * 0.7071067811865476))
    hidden = (pre * cdf).astype(jnp.bfloat16)
    out_t = lax.dot_general(w_out_t, hidden, (((1,), (1,)), ((), ())), preferred_element_type=jnp.float32)
    out_t = out_t.astype(out_ref.dtype)
    width = out_ref.shape[2]
    for s in range(slots):
        out_ref[s] = out_t[:, s * width:(s + 1) * width]
    grad_out_t = jnp.dot(g_t, hidden, preferred_element_type=jnp.float32)
    back = lax.dot_general(g_t, w_out_t, (((0,), (0,)), ((), ())), preferred_element_type=jnp.float32)
    slope = cdf + pre * jnp.exp(-0.5 * pre * pre) * 0.3989422804014327
    scaled = (back * slope).astype(jnp.bfloat16)
    grad_in = jnp.dot(x_t, scaled, preferred_element_type=jnp.float32)
    for c in range(grad_in.shape[1] // 128):
        flat_ref[0, c] = grad_in[:, c * 128:(c + 1) * 128]
        flat_ref[1, c] = grad_out_t[:, c * 128:(c + 1) * 128]


def run_experts(inputs, grads, w_in, w_out_t):
    experts, slots, channels, width = inputs.shape
    hidden = w_in.shape[2]
    pieces = hidden // 128
    tok = pl.BlockSpec((None, slots, channels, width), lambda e: (e, 0, 0, 0))
    weight = pl.BlockSpec((None, channels, hidden), lambda e: (e, 0, 0))
    return pl.pallas_call(
        expert_kernel,
        grid=(experts,),
        out_shape=[
            jax.ShapeDtypeStruct(inputs.shape, jnp.bfloat16),
            jax.ShapeDtypeStruct((experts, 2, pieces, channels, 128), jnp.float32),
        ],
        in_specs=[tok, tok, weight, weight],
        out_specs=[tok, pl.BlockSpec((None, 2, pieces, channels, 128), lambda e: (e, 0, 0, 0, 0))],
        compiler_params=pltpu.CompilerParams(vmem_limit_bytes=48 * 1024 * 1024),
    )(inputs, grads, w_in, w_out_t)

def gelu_slope(values):
    return (
        0.5 * (1.0 + lax.erf(values * 0.7071067811865476))
        + values * jnp.exp(-0.5 * values * values) * 0.3989422804014327
    )


def depthwise(padded, kernel):
    row_count = padded.shape[1] - 6
    col_count = padded.shape[2] - 6
    summed = jnp.zeros((padded.shape[0], row_count, col_count, padded.shape[3]), jnp.float32)
    for row_off in range(7):
        for col_off in range(7):
            window = padded[:, row_off : row_off + row_count, col_off : col_off + col_count, :]
            summed = summed + window.astype(jnp.float32) * kernel[row_off, col_off]
    return summed


def widen(picture):
    return jnp.pad(picture, ((0, 0), (0, 0), (3, 3), (0, 0)))


def dense_block(images, smoothed, ln_gain, w_expand, w_reduce):
    channels = images.shape[-1]
    channel_mean = jnp.mean(smoothed, axis=-1, keepdims=True)
    centered = smoothed - channel_mean
    variance = jnp.mean(centered * centered, axis=-1, keepdims=True)
    normed = (centered * lax.rsqrt(variance + 1e-06) * ln_gain).astype(jnp.bfloat16)
    flat_normed = normed.reshape(-1, channels)
    expanded = jnp.dot(flat_normed, w_expand, preferred_element_type=jnp.float32)
    active = jax.nn.gelu(expanded, approximate=False).astype(jnp.bfloat16)
    reduced = jnp.dot(active, w_reduce, preferred_element_type=jnp.float32)
    dense_out = images.reshape(-1, channels).astype(jnp.float32) + reduced
    return dense_out.astype(jnp.bfloat16).reshape(images.shape)


def expert_pass(inputs, grads_in, w_in, w_out):
    pre_act = jnp.dot(inputs, w_in, preferred_element_type=jnp.float32)
    hidden = jax.nn.gelu(pre_act, approximate=False).astype(jnp.bfloat16)
    outputs = jnp.dot(hidden, w_out, preferred_element_type=jnp.float32).astype(jnp.bfloat16)
    grad_out = jnp.dot(hidden.T, grads_in, preferred_element_type=jnp.float32)
    back_prop = jnp.dot(grads_in, w_out.T, preferred_element_type=jnp.float32)
    scaled = (back_prop * gelu_slope(pre_act)).astype(jnp.bfloat16)
    grad_in = jnp.dot(inputs.T, scaled, preferred_element_type=jnp.float32)
    return (outputs, grad_in, grad_out)


def body(images, cotangent, labels, dw_kernel, ln_gain, w_expand, w_reduce, exp_in, exp_out):
    channels = images.shape[-1]
    padded = with_halo(images, (("lat", 1),), 3)
    smoothed = depthwise(widen(padded), dw_kernel)
    dense_out = dense_block(images, smoothed, ln_gain, w_expand, w_reduce)
    rows, width = images.shape[1], images.shape[2]
    per_row = width // BLOCK

    def to_blocks(pixels):
        pixels = pixels.reshape(rows, per_row, BLOCK, channels)
        return jnp.transpose(pixels, (0, 1, 3, 2)).reshape(rows * per_row, channels, BLOCK)

    blocks = to_blocks(dense_out)
    grad_blocks = to_blocks(cotangent)
    flat_labels = labels.reshape(-1)
    members = (flat_labels[:, None] == jnp.arange(EXPERTS, dtype=jnp.int32)[None, :]).astype(
        jnp.int32
    )
    before = jnp.sum(jnp.cumsum(members, axis=0) * members, axis=1) - 1
    slot_of = flat_labels * CAP + before
    placer = jnp.arange(EXPERTS * CAP, dtype=jnp.int32)[:, None] == slot_of[None, :]
    block_of_slot = jnp.argmax(placer, axis=1)
    filled = jnp.any(placer, axis=1)[:, None, None]
    outgoing = blocks[block_of_slot].reshape(EXPERTS, CAP, channels, BLOCK)
    outgoing_grads = jnp.where(filled, grad_blocks[block_of_slot], jnp.zeros((), jnp.bfloat16)).reshape(
        EXPERTS, CAP, channels, BLOCK
    )
    arrived, arrived_grads = (
        lax.all_to_all(outgoing, "exp", split_axis=0, concat_axis=1, tiled=True),
        lax.all_to_all(outgoing_grads, "exp", split_axis=0, concat_axis=1, tiled=True),
    )
    local = arrived.shape[0]
    results, flat = run_experts(arrived, arrived_grads, exp_in, jnp.transpose(exp_out, (0, 2, 1)))
    returned = lax.all_to_all(results, "exp", split_axis=1, concat_axis=0, tiled=True)
    seg = reduce_scatter(flat.reshape(-1, 128))
    expert_blocks = returned.reshape(EXPERTS * CAP, channels, BLOCK)[slot_of]
    expert_out = jnp.transpose(expert_blocks.reshape(rows, per_row, channels, BLOCK), (0, 1, 3, 2))
    output = (
        dense_out.astype(jnp.float32) + expert_out.reshape(dense_out.shape).astype(jnp.float32)
    ).astype(jnp.bfloat16)
    rows_all = flat.size // 128
    grad_in, grad_out_t = all_gather(seg, output, rows_all, local, channels, exp_in.shape[2])
    grad_out = jnp.transpose(grad_out_t, (0, 2, 1))
    return (output, grad_in, grad_out)


def solution(mesh):
    in_specs = (
        P(("dp", "exp"), "lat", None, None),
        P(("dp", "exp"), "lat", None, None),
        P(("dp", "exp"), "lat", None, None),
        P(),
        P(),
        P(),
        P(),
        P("exp", None, None),
        P("exp", None, None),
    )
    out_specs = (P(("dp", "exp"), "lat", None, None), P("exp", None, None), P("exp", None, None))
    return jax.shard_map(body, mesh=mesh, in_specs=in_specs, out_specs=out_specs, check_vma=False)
```

```python
import jax
import jax.numpy as jnp
from jax import lax
from jax.sharding import PartitionSpec as P
from jax.experimental import pallas as pl
from jax.experimental.pallas import tpu as pltpu

EXPERTS = 16
BLOCK = 128
CAP = 3


def with_halo(block, sides, width):
    for axis, dim in sides:
        count = lax.axis_size(axis)
        forward = [(i, i + 1) for i in range(count - 1)]
        backward = [(target, source) for source, target in forward]
        low = lax.ppermute(
            lax.slice_in_dim(block, block.shape[dim] - width, None, axis=dim), axis, forward
        )
        high = lax.ppermute(lax.slice_in_dim(block, 0, width, axis=dim), axis, backward)
        block = jnp.concatenate([low, block, high], axis=dim)
    return block


def reduce_plan(lat_size, dp_size):
    dp_bits = dp_size.bit_length() - 1
    rest = list(range(1, dp_bits))
    other = rest[2:] + rest[:2] if len(rest) > 2 else rest
    plan = [("dp", 0, 0)] + [("dp", a, b) for a, b in zip(rest, other)]
    plan += [("lat", 0, 0)] * (lat_size.bit_length() - 1)
    return plan


def allreduce_kernel(plan, rows, in_ref, out_in, out_outt, *scratch):
    stages = len(plan)
    bufs = scratch[:stages]
    sums = scratch[stages:2 * stages]
    staged = scratch[2 * stages:3 * stages]
    gathered = scratch[3 * stages]
    rs_send, rs_recv, ag_send, ag_recv = scratch[3 * stages + 1:]
    lat = lax.axis_index("lat")
    dp = lax.axis_index("dp")
    ex = lax.axis_index("exp")
    core = dp % 2

    bits, partners = [], []
    for axis, b0, b1 in plan:
        me = dp if axis == "dp" else lat
        bit = jnp.where(core == 0, (me // (1 << b0)) % 2, (me // (1 << b1)) % 2)
        step = jnp.where(core == 0, 1 << b0, 1 << b1)
        other = me + (1 - 2 * bit) * step
        bits.append(bit)
        partners.append((lat, other, ex) if axis == "dp" else (other, dp, ex))

    barrier = pltpu.get_barrier_semaphore()
    for dev in partners:
        pl.semaphore_signal(barrier, 1, device_id=dev, device_id_type=pl.DeviceIdType.MESH)
    pl.semaphore_wait(barrier, stages)

    def chunked(count, body):
        chunk = min(count, 1152)
        lax.fori_loop(0, count // chunk, lambda i, c: (body(pl.multiple_of(i * chunk, 16), chunk), c)[1], 0)

    los = []
    lo = jnp.int32(0)
    for k in range(stages):
        half = rows >> (k + 1)
        los.append(lo)
        src = in_ref if k == 0 else sums[k - 1]
        keep = bits[k] * half
        give = (1 - bits[k]) * half

        def narrow(at, chunk, src=src, give=give, k=k):
            staged[k][pl.ds(at, chunk)] = src[pl.ds(pl.multiple_of(give + at, 16), chunk)].astype(jnp.bfloat16)

        def add(at, chunk, src=src, keep=keep, k=k):
            sums[k][pl.ds(at, chunk)] = src[pl.ds(pl.multiple_of(keep + at, 16), chunk)] + bufs[k][
                pl.ds(at, chunk)
            ].astype(jnp.float32)

        parts = 2 if half >= 576 else 1
        piece = half // parts
        copies = []
        for p in range(parts):
            lax.fori_loop(
                0,
                piece // min(piece, 1152),
                lambda i, c, p=p, narrow=narrow: (
                    narrow(pl.multiple_of(p * piece + i * min(piece, 1152), 16), min(piece, 1152)),
                    c,
                )[1],
                0,
            )
            copy = pltpu.make_async_remote_copy(
                src_ref=staged[k].at[pl.ds(p * piece, piece)],
                dst_ref=bufs[k].at[pl.ds(p * piece, piece)],
                send_sem=rs_send.at[2 * k + p],
                recv_sem=rs_recv.at[2 * k + p],
                device_id=partners[k],
                device_id_type=pl.DeviceIdType.MESH,
            )
            copy.start()
            copies.append(copy)
        for p in range(parts):
            copies[p].wait()
            lax.fori_loop(
                0,
                piece // min(piece, 1152),
                lambda i, c, p=p, add=add: (
                    add(pl.multiple_of(p * piece + i * min(piece, 1152), 16), min(piece, 1152)),
                    c,
                )[1],
                0,
            )
        lo = lo + bits[k] * half

    last = rows >> stages
    lo = pl.multiple_of(lo, 16)
    gathered[pl.ds(lo, last)] = sums[stages - 1][...].astype(jnp.bfloat16)
    for k in reversed(range(stages)):
        half = rows >> (k + 1)
        copy = pltpu.make_async_remote_copy(
            src_ref=gathered.at[pl.ds(pl.multiple_of(lo, 16), half)],
            dst_ref=gathered.at[pl.ds(pl.multiple_of(lo, 16), half)],
            send_sem=ag_send.at[k],
            recv_sem=ag_recv.at[k],
            device_id=partners[k],
            device_id_type=pl.DeviceIdType.MESH,
        )
        copy.start()
        copy.wait()
        lo = los[k]

    experts, channels, hidden = out_in.shape
    pieces = hidden // 128
    for e in range(experts):
        for t, dst in enumerate((out_in, out_outt)):
            for c in range(pieces):
                at = ((e * 2 + t) * pieces + c) * channels
                dst[e, :, c * 128:(c + 1) * 128] = gathered[at:at + channels].astype(jnp.float32)


def tree_allreduce(flat, experts, channels, hidden):
    rows = flat.shape[0]
    plan = reduce_plan(lax.axis_size("lat"), lax.axis_size("dp"))
    stages = len(plan)
    scratch = [pltpu.VMEM((rows >> (k + 1), 128), jnp.bfloat16) for k in range(stages)]
    scratch += [pltpu.VMEM((rows >> (k + 1), 128), jnp.float32) for k in range(stages)]
    scratch += [pltpu.VMEM((rows >> (k + 1), 128), jnp.bfloat16) for k in range(stages)]
    scratch += [pltpu.VMEM((rows, 128), jnp.bfloat16)]
    scratch += [pltpu.SemaphoreType.DMA((2 * stages,))] * 2 + [pltpu.SemaphoreType.DMA((stages,))] * 2
    return pl.pallas_call(
        lambda *refs: allreduce_kernel(plan, rows, *refs),
        out_shape=[jax.ShapeDtypeStruct((experts, channels, hidden), jnp.float32)] * 2,
        in_specs=[pl.BlockSpec(memory_space=pltpu.VMEM)],
        out_specs=[pl.BlockSpec(memory_space=pltpu.VMEM)] * 2,
        scratch_shapes=scratch,
        compiler_params=pltpu.CompilerParams(
            collective_id=0, has_side_effects=True, vmem_limit_bytes=62 * 1024 * 1024
        ),
    )(flat)

def expert_kernel(x_ref, g_ref, win_ref, wout_ref, out_ref, flat_ref):
    slots = x_ref.shape[0]
    x_t = jnp.concatenate([x_ref[s] for s in range(slots)], axis=1)
    g_t = jnp.concatenate([g_ref[s] for s in range(slots)], axis=1)
    w_out_t = wout_ref[...]
    pre = lax.dot_general(x_t, win_ref[...], (((0,), (0,)), ((), ())), preferred_element_type=jnp.float32)
    cdf = 0.5 * (1.0 + lax.erf(pre * 0.7071067811865476))
    hidden = (pre * cdf).astype(jnp.bfloat16)
    out_t = lax.dot_general(w_out_t, hidden, (((1,), (1,)), ((), ())), preferred_element_type=jnp.float32)
    out_t = out_t.astype(out_ref.dtype)
    width = out_ref.shape[2]
    for s in range(slots):
        out_ref[s] = out_t[:, s * width:(s + 1) * width]
    grad_out_t = jnp.dot(g_t, hidden, preferred_element_type=jnp.float32)
    back = lax.dot_general(g_t, w_out_t, (((0,), (0,)), ((), ())), preferred_element_type=jnp.float32)
    slope = cdf + pre * jnp.exp(-0.5 * pre * pre) * 0.3989422804014327
    scaled = (back * slope).astype(jnp.bfloat16)
    grad_in = jnp.dot(x_t, scaled, preferred_element_type=jnp.float32)
    for c in range(grad_in.shape[1] // 128):
        flat_ref[0, c] = grad_in[:, c * 128:(c + 1) * 128]
        flat_ref[1, c] = grad_out_t[:, c * 128:(c + 1) * 128]


def run_experts(inputs, grads, w_in, w_out_t):
    experts, slots, channels, width = inputs.shape
    hidden = w_in.shape[2]
    pieces = hidden // 128
    tok = pl.BlockSpec((None, slots, channels, width), lambda e: (e, 0, 0, 0))
    weight = pl.BlockSpec((None, channels, hidden), lambda e: (e, 0, 0))
    return pl.pallas_call(
        expert_kernel,
        grid=(experts,),
        out_shape=[
            jax.ShapeDtypeStruct(inputs.shape, jnp.bfloat16),
            jax.ShapeDtypeStruct((experts, 2, pieces, channels, 128), jnp.float32),
        ],
        in_specs=[tok, tok, weight, weight],
        out_specs=[tok, pl.BlockSpec((None, 2, pieces, channels, 128), lambda e: (e, 0, 0, 0, 0))],
        compiler_params=pltpu.CompilerParams(vmem_limit_bytes=48 * 1024 * 1024),
    )(inputs, grads, w_in, w_out_t)

def gelu_slope(values):
    return (
        0.5 * (1.0 + lax.erf(values * 0.7071067811865476))
        + values * jnp.exp(-0.5 * values * values) * 0.3989422804014327
    )


def depthwise(padded, kernel):
    row_count = padded.shape[1] - 6
    col_count = padded.shape[2] - 6
    summed = jnp.zeros((padded.shape[0], row_count, col_count, padded.shape[3]), jnp.float32)
    for row_off in range(7):
        for col_off in range(7):
            window = padded[:, row_off : row_off + row_count, col_off : col_off + col_count, :]
            summed = summed + window.astype(jnp.float32) * kernel[row_off, col_off]
    return summed


def widen(picture):
    return jnp.pad(picture, ((0, 0), (0, 0), (3, 3), (0, 0)))


def dense_block(images, smoothed, ln_gain, w_expand, w_reduce):
    channels = images.shape[-1]
    channel_mean = jnp.mean(smoothed, axis=-1, keepdims=True)
    centered = smoothed - channel_mean
    variance = jnp.mean(centered * centered, axis=-1, keepdims=True)
    normed = (centered * lax.rsqrt(variance + 1e-06) * ln_gain).astype(jnp.bfloat16)
    flat_normed = normed.reshape(-1, channels)
    expanded = jnp.dot(flat_normed, w_expand, preferred_element_type=jnp.float32)
    active = jax.nn.gelu(expanded, approximate=False).astype(jnp.bfloat16)
    reduced = jnp.dot(active, w_reduce, preferred_element_type=jnp.float32)
    dense_out = images.reshape(-1, channels).astype(jnp.float32) + reduced
    return dense_out.astype(jnp.bfloat16).reshape(images.shape)


def expert_pass(inputs, grads_in, w_in, w_out):
    pre_act = jnp.dot(inputs, w_in, preferred_element_type=jnp.float32)
    hidden = jax.nn.gelu(pre_act, approximate=False).astype(jnp.bfloat16)
    outputs = jnp.dot(hidden, w_out, preferred_element_type=jnp.float32).astype(jnp.bfloat16)
    grad_out = jnp.dot(hidden.T, grads_in, preferred_element_type=jnp.float32)
    back_prop = jnp.dot(grads_in, w_out.T, preferred_element_type=jnp.float32)
    scaled = (back_prop * gelu_slope(pre_act)).astype(jnp.bfloat16)
    grad_in = jnp.dot(inputs.T, scaled, preferred_element_type=jnp.float32)
    return (outputs, grad_in, grad_out)


def body(images, cotangent, labels, dw_kernel, ln_gain, w_expand, w_reduce, exp_in, exp_out):
    channels = images.shape[-1]
    padded = with_halo(images, (("lat", 1),), 3)
    smoothed = depthwise(widen(padded), dw_kernel)
    dense_out = dense_block(images, smoothed, ln_gain, w_expand, w_reduce)
    rows, width = images.shape[1], images.shape[2]
    per_row = width // BLOCK

    def to_blocks(pixels):
        pixels = pixels.reshape(rows, per_row, BLOCK, channels)
        return jnp.transpose(pixels, (0, 1, 3, 2)).reshape(rows * per_row, channels, BLOCK)

    blocks = to_blocks(dense_out)
    grad_blocks = to_blocks(cotangent)
    flat_labels = labels.reshape(-1)
    members = (flat_labels[:, None] == jnp.arange(EXPERTS, dtype=jnp.int32)[None, :]).astype(
        jnp.int32
    )
    before = jnp.sum(jnp.cumsum(members, axis=0) * members, axis=1) - 1
    slot_of = flat_labels * CAP + before
    placer = jnp.arange(EXPERTS * CAP, dtype=jnp.int32)[:, None] == slot_of[None, :]
    block_of_slot = jnp.argmax(placer, axis=1)
    filled = jnp.any(placer, axis=1)[:, None, None]
    outgoing = blocks[block_of_slot].reshape(EXPERTS, CAP, channels, BLOCK)
    outgoing_grads = jnp.where(filled, grad_blocks[block_of_slot], jnp.zeros((), jnp.bfloat16)).reshape(
        EXPERTS, CAP, channels, BLOCK
    )
    arrived, arrived_grads = (
        lax.all_to_all(outgoing, "exp", split_axis=0, concat_axis=1, tiled=True),
        lax.all_to_all(outgoing_grads, "exp", split_axis=0, concat_axis=1, tiled=True),
    )
    local = arrived.shape[0]
    results, flat = run_experts(arrived, arrived_grads, exp_in, jnp.transpose(exp_out, (0, 2, 1)))
    returned = lax.all_to_all(results, "exp", split_axis=1, concat_axis=0, tiled=True)
    grad_in, grad_out_t = tree_allreduce(flat.reshape(-1, 128), local, channels, exp_in.shape[2])
    grad_out = jnp.transpose(grad_out_t, (0, 2, 1))
    expert_blocks = returned.reshape(EXPERTS * CAP, channels, BLOCK)[slot_of]
    expert_out = jnp.transpose(expert_blocks.reshape(rows, per_row, channels, BLOCK), (0, 1, 3, 2))
    output = (
        dense_out.astype(jnp.float32) + expert_out.reshape(dense_out.shape).astype(jnp.float32)
    ).astype(jnp.bfloat16)
    return (output, grad_in, grad_out)


def solution(mesh):
    in_specs = (
        P(("dp", "exp"), "lat", None, None),
        P(("dp", "exp"), "lat", None, None),
        P(("dp", "exp"), "lat", None, None),
        P(),
        P(),
        P(),
        P(),
        P("exp", None, None),
        P("exp", None, None),
    )
    out_specs = (P(("dp", "exp"), "lat", None, None), P("exp", None, None), P("exp", None, None))
    return jax.shard_map(body, mesh=mesh, in_specs=in_specs, out_specs=out_specs, check_vma=False)
```

```python
import jax
import jax.numpy as jnp
from jax import lax
from jax.sharding import PartitionSpec as P
from jax.experimental import pallas as pl
from jax.experimental.pallas import tpu as pltpu

EXPERTS = 16
BLOCK = 128
CAP = 3


def with_halo(block, sides, width):
    for axis, dim in sides:
        count = lax.axis_size(axis)
        forward = [(i, i + 1) for i in range(count - 1)]
        backward = [(target, source) for source, target in forward]
        low = lax.ppermute(
            lax.slice_in_dim(block, block.shape[dim] - width, None, axis=dim), axis, forward
        )
        high = lax.ppermute(lax.slice_in_dim(block, 0, width, axis=dim), axis, backward)
        block = jnp.concatenate([low, block, high], axis=dim)
    return block


def reduce_plan(lat_size, dp_size):
    dp_bits = dp_size.bit_length() - 1
    rest = list(range(1, dp_bits))
    other = rest[2:] + rest[:2] if len(rest) > 2 else rest
    plan = [("dp", 0, 0)] + [("dp", a, b) for a, b in zip(rest, other)]
    plan += [("lat", 0, 0)] * (lat_size.bit_length() - 1)
    return plan


def allreduce_kernel(plan, rows, in_ref, out_in, out_outt, *scratch):
    stages = len(plan)
    bufs = scratch[:stages]
    sums = scratch[stages:2 * stages]
    staged = scratch[2 * stages:3 * stages]
    gathered = scratch[3 * stages]
    rs_send, rs_recv, ag_send, ag_recv = scratch[3 * stages + 1:]
    lat = lax.axis_index("lat")
    dp = lax.axis_index("dp")
    ex = lax.axis_index("exp")
    core = dp % 2

    bits, partners = [], []
    for axis, b0, b1 in plan:
        me = dp if axis == "dp" else lat
        bit = jnp.where(core == 0, (me // (1 << b0)) % 2, (me // (1 << b1)) % 2)
        step = jnp.where(core == 0, 1 << b0, 1 << b1)
        other = me + (1 - 2 * bit) * step
        bits.append(bit)
        partners.append((lat, other, ex) if axis == "dp" else (other, dp, ex))

    barrier = pltpu.get_barrier_semaphore()
    for dev in partners:
        pl.semaphore_signal(barrier, 1, device_id=dev, device_id_type=pl.DeviceIdType.MESH)
    pl.semaphore_wait(barrier, stages)

    def chunked(count, body):
        chunk = min(count, 1152)
        lax.fori_loop(0, count // chunk, lambda i, c: (body(pl.multiple_of(i * chunk, 16), chunk), c)[1], 0)

    los = []
    lo = jnp.int32(0)
    for k in range(stages):
        half = rows >> (k + 1)
        los.append(lo)
        src = in_ref if k == 0 else sums[k - 1]
        keep = bits[k] * half
        give = (1 - bits[k]) * half

        def narrow(at, chunk, src=src, give=give, k=k):
            staged[k][pl.ds(at, chunk)] = src[pl.ds(pl.multiple_of(give + at, 16), chunk)].astype(jnp.bfloat16)

        def add(at, chunk, src=src, keep=keep, k=k):
            sums[k][pl.ds(at, chunk)] = src[pl.ds(pl.multiple_of(keep + at, 16), chunk)] + bufs[k][
                pl.ds(at, chunk)
            ].astype(jnp.float32)

        parts = 2 if half >= 576 else 1
        piece = half // parts
        copies = []
        for p in range(parts):
            lax.fori_loop(
                0,
                piece // min(piece, 1152),
                lambda i, c, p=p, narrow=narrow: (
                    narrow(pl.multiple_of(p * piece + i * min(piece, 1152), 16), min(piece, 1152)),
                    c,
                )[1],
                0,
            )
            copy = pltpu.make_async_remote_copy(
                src_ref=staged[k].at[pl.ds(p * piece, piece)],
                dst_ref=bufs[k].at[pl.ds(p * piece, piece)],
                send_sem=rs_send.at[2 * k + p],
                recv_sem=rs_recv.at[2 * k + p],
                device_id=partners[k],
                device_id_type=pl.DeviceIdType.MESH,
            )
            copy.start()
            copies.append(copy)
        for p in range(parts):
            copies[p].wait()
            lax.fori_loop(
                0,
                piece // min(piece, 1152),
                lambda i, c, p=p, add=add: (
                    add(pl.multiple_of(p * piece + i * min(piece, 1152), 16), min(piece, 1152)),
                    c,
                )[1],
                0,
            )
        lo = lo + bits[k] * half

    last = rows >> stages
    lo = pl.multiple_of(lo, 16)
    gathered[pl.ds(lo, last)] = sums[stages - 1][...].astype(jnp.bfloat16)
    for k in reversed(range(stages)):
        half = rows >> (k + 1)
        copy = pltpu.make_async_remote_copy(
            src_ref=gathered.at[pl.ds(pl.multiple_of(lo, 16), half)],
            dst_ref=gathered.at[pl.ds(pl.multiple_of(lo, 16), half)],
            send_sem=ag_send.at[k],
            recv_sem=ag_recv.at[k],
            device_id=partners[k],
            device_id_type=pl.DeviceIdType.MESH,
        )
        copy.start()
        copy.wait()
        lo = los[k]

    experts, channels, hidden = out_in.shape
    pieces = hidden // 128
    for e in range(experts):
        for t, dst in enumerate((out_in, out_outt)):
            for c in range(pieces):
                at = ((e * 2 + t) * pieces + c) * channels
                dst[e, :, c * 128:(c + 1) * 128] = gathered[at:at + channels].astype(jnp.float32)


def tree_allreduce(flat, experts, channels, hidden):
    rows = flat.shape[0]
    plan = reduce_plan(lax.axis_size("lat"), lax.axis_size("dp"))
    stages = len(plan)
    scratch = [pltpu.VMEM((rows >> (k + 1), 128), jnp.bfloat16) for k in range(stages)]
    scratch += [pltpu.VMEM((rows >> (k + 1), 128), jnp.float32) for k in range(stages)]
    scratch += [pltpu.VMEM((rows >> (k + 1), 128), jnp.bfloat16) for k in range(stages)]
    scratch += [pltpu.VMEM((rows, 128), jnp.bfloat16)]
    scratch += [pltpu.SemaphoreType.DMA((2 * stages,))] * 2 + [pltpu.SemaphoreType.DMA((stages,))] * 2
    return pl.pallas_call(
        lambda *refs: allreduce_kernel(plan, rows, *refs),
        out_shape=[jax.ShapeDtypeStruct((experts, channels, hidden), jnp.float32)] * 2,
        in_specs=[pl.BlockSpec(memory_space=pltpu.VMEM)],
        out_specs=[pl.BlockSpec(memory_space=pltpu.VMEM)] * 2,
        scratch_shapes=scratch,
        compiler_params=pltpu.CompilerParams(
            collective_id=0, has_side_effects=True, vmem_limit_bytes=62 * 1024 * 1024
        ),
    )(flat)

def expert_kernel(x_ref, g_ref, win_ref, wout_ref, *refs):
    if len(refs) == 3:
        prior_ref, out_ref, flat_ref = refs
    else:
        prior_ref = None
        out_ref, flat_ref = refs
    slots = x_ref.shape[0]
    x_t = jnp.concatenate([x_ref[s] for s in range(slots)], axis=1)
    g_t = jnp.concatenate([g_ref[s] for s in range(slots)], axis=1)
    w_out_t = wout_ref[...]
    pre = lax.dot_general(x_t, win_ref[...], (((0,), (0,)), ((), ())), preferred_element_type=jnp.float32)
    cdf = 0.5 * (1.0 + lax.erf(pre * 0.7071067811865476))
    hidden = (pre * cdf).astype(jnp.bfloat16)
    out_t = lax.dot_general(w_out_t, hidden, (((1,), (1,)), ((), ())), preferred_element_type=jnp.float32)
    out_t = out_t.astype(out_ref.dtype)
    width = out_ref.shape[2]
    for s in range(slots):
        out_ref[s] = out_t[:, s * width:(s + 1) * width]
    grad_out_t = jnp.dot(g_t, hidden, preferred_element_type=jnp.float32)
    back = lax.dot_general(g_t, w_out_t, (((0,), (0,)), ((), ())), preferred_element_type=jnp.float32)
    slope = cdf + pre * jnp.exp(-0.5 * pre * pre) * 0.3989422804014327
    scaled = (back * slope).astype(jnp.bfloat16)
    grad_in = jnp.dot(x_t, scaled, preferred_element_type=jnp.float32)
    for c in range(grad_in.shape[1] // 128):
        gi = grad_in[:, c * 128:(c + 1) * 128]
        go = grad_out_t[:, c * 128:(c + 1) * 128]
        if prior_ref is not None:
            gi = gi + prior_ref[0, c]
            go = go + prior_ref[1, c]
        flat_ref[0, c] = gi
        flat_ref[1, c] = go


def run_experts(inputs, grads, w_in, w_out_t, prior=None):
    experts, slots, channels, width = inputs.shape
    hidden = w_in.shape[2]
    pieces = hidden // 128
    tok = pl.BlockSpec((None, slots, channels, width), lambda e: (e, 0, 0, 0))
    weight = pl.BlockSpec((None, channels, hidden), lambda e: (e, 0, 0))
    grad_spec = pl.BlockSpec((None, 2, pieces, channels, 128), lambda e: (e, 0, 0, 0, 0))
    operands = (inputs, grads, w_in, w_out_t) + (() if prior is None else (prior,))
    return pl.pallas_call(
        expert_kernel,
        grid=(experts,),
        out_shape=[
            jax.ShapeDtypeStruct(inputs.shape, jnp.bfloat16),
            jax.ShapeDtypeStruct((experts, 2, pieces, channels, 128), jnp.float32),
        ],
        in_specs=[tok, tok, weight, weight] + ([] if prior is None else [grad_spec]),
        out_specs=[tok, grad_spec],
        input_output_aliases={} if prior is None else {4: 1},
        compiler_params=pltpu.CompilerParams(vmem_limit_bytes=48 * 1024 * 1024),
    )(*operands)

def gelu_slope(values):
    return (
        0.5 * (1.0 + lax.erf(values * 0.7071067811865476))
        + values * jnp.exp(-0.5 * values * values) * 0.3989422804014327
    )


def depthwise(padded, kernel):
    row_count = padded.shape[1] - 6
    col_count = padded.shape[2] - 6
    summed = jnp.zeros((padded.shape[0], row_count, col_count, padded.shape[3]), jnp.float32)
    for row_off in range(7):
        for col_off in range(7):
            window = padded[:, row_off : row_off + row_count, col_off : col_off + col_count, :]
            summed = summed + window.astype(jnp.float32) * kernel[row_off, col_off]
    return summed


def widen(picture):
    return jnp.pad(picture, ((0, 0), (0, 0), (3, 3), (0, 0)))


def dense_block(images, smoothed, ln_gain, w_expand, w_reduce):
    channels = images.shape[-1]
    channel_mean = jnp.mean(smoothed, axis=-1, keepdims=True)
    centered = smoothed - channel_mean
    variance = jnp.mean(centered * centered, axis=-1, keepdims=True)
    normed = (centered * lax.rsqrt(variance + 1e-06) * ln_gain).astype(jnp.bfloat16)
    flat_normed = normed.reshape(-1, channels)
    expanded = jnp.dot(flat_normed, w_expand, preferred_element_type=jnp.float32)
    active = jax.nn.gelu(expanded, approximate=False).astype(jnp.bfloat16)
    reduced = jnp.dot(active, w_reduce, preferred_element_type=jnp.float32)
    dense_out = images.reshape(-1, channels).astype(jnp.float32) + reduced
    return dense_out.astype(jnp.bfloat16).reshape(images.shape)


def expert_pass(inputs, grads_in, w_in, w_out):
    pre_act = jnp.dot(inputs, w_in, preferred_element_type=jnp.float32)
    hidden = jax.nn.gelu(pre_act, approximate=False).astype(jnp.bfloat16)
    outputs = jnp.dot(hidden, w_out, preferred_element_type=jnp.float32).astype(jnp.bfloat16)
    grad_out = jnp.dot(hidden.T, grads_in, preferred_element_type=jnp.float32)
    back_prop = jnp.dot(grads_in, w_out.T, preferred_element_type=jnp.float32)
    scaled = (back_prop * gelu_slope(pre_act)).astype(jnp.bfloat16)
    grad_in = jnp.dot(inputs.T, scaled, preferred_element_type=jnp.float32)
    return (outputs, grad_in, grad_out)


def body(images, cotangent, labels, dw_kernel, ln_gain, w_expand, w_reduce, exp_in, exp_out):
    channels = images.shape[-1]
    padded = with_halo(images, (("lat", 1),), 3)
    smoothed = depthwise(widen(padded), dw_kernel)
    dense_out = dense_block(images, smoothed, ln_gain, w_expand, w_reduce)
    rows, width = images.shape[1], images.shape[2]
    per_row = width // BLOCK

    def to_blocks(pixels):
        pixels = pixels.reshape(rows, per_row, BLOCK, channels)
        return jnp.transpose(pixels, (0, 1, 3, 2)).reshape(rows * per_row, channels, BLOCK)

    blocks = to_blocks(dense_out)
    grad_blocks = to_blocks(cotangent)
    flat_labels = labels.reshape(-1)
    members = (flat_labels[:, None] == jnp.arange(EXPERTS, dtype=jnp.int32)[None, :]).astype(
        jnp.int32
    )
    before = jnp.sum(jnp.cumsum(members, axis=0) * members, axis=1) - 1
    slot_of = flat_labels * CAP + before
    placer = jnp.arange(EXPERTS * CAP, dtype=jnp.int32)[:, None] == slot_of[None, :]
    block_of_slot = jnp.argmax(placer, axis=1)
    filled = jnp.any(placer, axis=1)[:, None, None]
    outgoing = blocks[block_of_slot].reshape(EXPERTS, CAP, channels, BLOCK)
    outgoing_grads = jnp.where(filled, grad_blocks[block_of_slot], jnp.zeros((), jnp.bfloat16)).reshape(
        EXPERTS, CAP, channels, BLOCK
    )
    arrived, arrived_grads = (
        lax.all_to_all(outgoing, "exp", split_axis=0, concat_axis=1, tiled=True),
        lax.all_to_all(outgoing_grads, "exp", split_axis=0, concat_axis=1, tiled=True),
    )
    local = arrived.shape[0]
    me = lax.axis_index("exp")
    w_out_t = jnp.transpose(exp_out, (0, 2, 1))
    own = lax.dynamic_slice_in_dim(outgoing, me * local, local, axis=0)
    own_grads = lax.dynamic_slice_in_dim(outgoing_grads, me * local, local, axis=0)
    own_results, flat = run_experts(own, own_grads, exp_in, w_out_t)
    other = 1 - me
    far = lax.dynamic_slice_in_dim(arrived, other * CAP, CAP, axis=1)
    far_grads = lax.dynamic_slice_in_dim(arrived_grads, other * CAP, CAP, axis=1)
    far_results, flat = run_experts(far, far_grads, exp_in, w_out_t, flat)
    results = jnp.where(
        me == 0,
        jnp.concatenate([own_results, far_results], axis=1),
        jnp.concatenate([far_results, own_results], axis=1),
    )
    returned = lax.all_to_all(results, "exp", split_axis=1, concat_axis=0, tiled=True)
    grad_in, grad_out_t = tree_allreduce(flat.reshape(-1, 128), local, channels, exp_in.shape[2])
    grad_out = jnp.transpose(grad_out_t, (0, 2, 1))
    expert_blocks = returned.reshape(EXPERTS * CAP, channels, BLOCK)[slot_of]
    expert_out = jnp.transpose(expert_blocks.reshape(rows, per_row, channels, BLOCK), (0, 1, 3, 2))
    output = (
        dense_out.astype(jnp.float32) + expert_out.reshape(dense_out.shape).astype(jnp.float32)
    ).astype(jnp.bfloat16)
    return (output, grad_in, grad_out)


def solution(mesh):
    in_specs = (
        P(("dp", "exp"), "lat", None, None),
        P(("dp", "exp"), "lat", None, None),
        P(("dp", "exp"), "lat", None, None),
        P(),
        P(),
        P(),
        P(),
        P("exp", None, None),
        P("exp", None, None),
    )
    out_specs = (P(("dp", "exp"), "lat", None, None), P("exp", None, None), P("exp", None, None))
    return jax.shard_map(body, mesh=mesh, in_specs=in_specs, out_specs=out_specs, check_vma=False)
```

```python
import jax
import jax.numpy as jnp
from jax import lax
from jax.sharding import PartitionSpec as P
from jax.experimental import pallas as pl
from jax.experimental.pallas import tpu as pltpu

EXPERTS = 16
BLOCK = 128
CAP = 3


def with_halo(block, sides, width):
    for axis, dim in sides:
        count = lax.axis_size(axis)
        forward = [(i, i + 1) for i in range(count - 1)]
        backward = [(target, source) for source, target in forward]
        low = lax.ppermute(
            lax.slice_in_dim(block, block.shape[dim] - width, None, axis=dim), axis, forward
        )
        high = lax.ppermute(lax.slice_in_dim(block, 0, width, axis=dim), axis, backward)
        block = jnp.concatenate([low, block, high], axis=dim)
    return block


def reduce_plan(lat_size, dp_size):
    dp_bits = dp_size.bit_length() - 1
    rest = list(range(1, dp_bits))
    other = rest[2:] + rest[:2] if len(rest) > 2 else rest
    plan = [("dp", 0, 0)] + [("dp", a, b) for a, b in zip(rest, other)]
    plan += [("lat", 0, 0)] * (lat_size.bit_length() - 1)
    return plan


def allreduce_kernel(plan, rows, in_ref, out_in, out_outt, *scratch):
    stages = len(plan)
    bufs = scratch[:stages]
    sums = scratch[stages:2 * stages]
    staged = scratch[2 * stages:3 * stages]
    gathered = scratch[3 * stages]
    rs_send, rs_recv, ag_send, ag_recv = scratch[3 * stages + 1:]
    lat = lax.axis_index("lat")
    dp = lax.axis_index("dp")
    ex = lax.axis_index("exp")
    core = dp % 2

    bits, partners = [], []
    for axis, b0, b1 in plan:
        me = dp if axis == "dp" else lat
        bit = jnp.where(core == 0, (me // (1 << b0)) % 2, (me // (1 << b1)) % 2)
        step = jnp.where(core == 0, 1 << b0, 1 << b1)
        other = me + (1 - 2 * bit) * step
        bits.append(bit)
        partners.append((lat, other, ex) if axis == "dp" else (other, dp, ex))

    barrier = pltpu.get_barrier_semaphore()
    for dev in partners:
        pl.semaphore_signal(barrier, 1, device_id=dev, device_id_type=pl.DeviceIdType.MESH)
    pl.semaphore_wait(barrier, stages)

    def chunked(count, body):
        chunk = min(count, 1152)
        lax.fori_loop(0, count // chunk, lambda i, c: (body(pl.multiple_of(i * chunk, 16), chunk), c)[1], 0)

    los = []
    lo = jnp.int32(0)
    for k in range(stages):
        half = rows >> (k + 1)
        los.append(lo)
        src = in_ref if k == 0 else sums[k - 1]
        keep = bits[k] * half
        give = (1 - bits[k]) * half

        def narrow(at, chunk, src=src, give=give, k=k):
            staged[k][pl.ds(at, chunk)] = src[pl.ds(pl.multiple_of(give + at, 16), chunk)].astype(jnp.bfloat16)

        def add(at, chunk, src=src, keep=keep, k=k):
            sums[k][pl.ds(at, chunk)] = src[pl.ds(pl.multiple_of(keep + at, 16), chunk)] + bufs[k][
                pl.ds(at, chunk)
            ].astype(jnp.float32)

        parts = 2 if half >= 576 else 1
        piece = half // parts
        copies = []
        for p in range(parts):
            lax.fori_loop(
                0,
                piece // min(piece, 1152),
                lambda i, c, p=p, narrow=narrow: (
                    narrow(pl.multiple_of(p * piece + i * min(piece, 1152), 16), min(piece, 1152)),
                    c,
                )[1],
                0,
            )
            copy = pltpu.make_async_remote_copy(
                src_ref=staged[k].at[pl.ds(p * piece, piece)],
                dst_ref=bufs[k].at[pl.ds(p * piece, piece)],
                send_sem=rs_send.at[2 * k + p],
                recv_sem=rs_recv.at[2 * k + p],
                device_id=partners[k],
                device_id_type=pl.DeviceIdType.MESH,
            )
            copy.start()
            copies.append(copy)
        for p in range(parts):
            copies[p].wait()
            lax.fori_loop(
                0,
                piece // min(piece, 1152),
                lambda i, c, p=p, add=add: (
                    add(pl.multiple_of(p * piece + i * min(piece, 1152), 16), min(piece, 1152)),
                    c,
                )[1],
                0,
            )
        lo = lo + bits[k] * half

    last = rows >> stages
    lo = pl.multiple_of(lo, 16)
    gathered[pl.ds(lo, last)] = sums[stages - 1][...].astype(jnp.bfloat16)
    for k in reversed(range(stages)):
        half = rows >> (k + 1)
        copy = pltpu.make_async_remote_copy(
            src_ref=gathered.at[pl.ds(pl.multiple_of(lo, 16), half)],
            dst_ref=gathered.at[pl.ds(pl.multiple_of(lo, 16), half)],
            send_sem=ag_send.at[k],
            recv_sem=ag_recv.at[k],
            device_id=partners[k],
            device_id_type=pl.DeviceIdType.MESH,
        )
        copy.start()
        copy.wait()
        lo = los[k]

    experts, channels, hidden = out_in.shape
    pieces = hidden // 128
    for e in range(experts):
        for t, dst in enumerate((out_in, out_outt)):
            for c in range(pieces):
                at = ((e * 2 + t) * pieces + c) * channels
                dst[e, :, c * 128:(c + 1) * 128] = gathered[at:at + channels].astype(jnp.float32)


def tree_allreduce(flat, experts, channels, hidden):
    rows = flat.shape[0]
    plan = reduce_plan(lax.axis_size("lat"), lax.axis_size("dp"))
    stages = len(plan)
    scratch = [pltpu.VMEM((rows >> (k + 1), 128), jnp.bfloat16) for k in range(stages)]
    scratch += [pltpu.VMEM((rows >> (k + 1), 128), jnp.float32) for k in range(stages)]
    scratch += [pltpu.VMEM((rows >> (k + 1), 128), jnp.bfloat16) for k in range(stages)]
    scratch += [pltpu.VMEM((rows, 128), jnp.bfloat16)]
    scratch += [pltpu.SemaphoreType.DMA((2 * stages,))] * 2 + [pltpu.SemaphoreType.DMA((stages,))] * 2
    return pl.pallas_call(
        lambda *refs: allreduce_kernel(plan, rows, *refs),
        out_shape=[jax.ShapeDtypeStruct((experts, channels, hidden), jnp.float32)] * 2,
        in_specs=[pl.BlockSpec(memory_space=pltpu.VMEM)],
        out_specs=[pl.BlockSpec(memory_space=pltpu.VMEM)] * 2,
        scratch_shapes=scratch,
        compiler_params=pltpu.CompilerParams(
            collective_id=0, has_side_effects=True, vmem_limit_bytes=62 * 1024 * 1024
        ),
    )(flat)

def expert_kernel(x_ref, g_ref, win_ref, wout_ref, out_ref, flat_ref):
    slots = x_ref.shape[0]
    x_t = jnp.concatenate([x_ref[s] for s in range(slots)], axis=1)
    g_t = jnp.concatenate([g_ref[s] for s in range(slots)], axis=1)
    w_out_t = wout_ref[...]
    pre = lax.dot_general(x_t, win_ref[...], (((0,), (0,)), ((), ())), preferred_element_type=jnp.float32)
    cdf = 0.5 * (1.0 + lax.erf(pre * 0.7071067811865476))
    hidden = (pre * cdf).astype(jnp.bfloat16)
    out_t = lax.dot_general(w_out_t, hidden, (((1,), (1,)), ((), ())), preferred_element_type=jnp.float32)
    out_t = out_t.astype(out_ref.dtype)
    width = out_ref.shape[2]
    for s in range(slots):
        out_ref[s] = out_t[:, s * width:(s + 1) * width]
    grad_out_t = jnp.dot(g_t, hidden, preferred_element_type=jnp.float32)
    back = lax.dot_general(g_t, w_out_t, (((0,), (0,)), ((), ())), preferred_element_type=jnp.float32)
    slope = cdf + pre * jnp.exp(-0.5 * pre * pre) * 0.3989422804014327
    scaled = (back * slope).astype(jnp.bfloat16)
    grad_in = jnp.dot(x_t, scaled, preferred_element_type=jnp.float32)
    for c in range(grad_in.shape[1] // 128):
        flat_ref[0, c] = grad_in[:, c * 128:(c + 1) * 128]
        flat_ref[1, c] = grad_out_t[:, c * 128:(c + 1) * 128]


def run_experts(inputs, grads, w_in, w_out_t):
    experts, slots, channels, width = inputs.shape
    hidden = w_in.shape[2]
    pieces = hidden // 128
    tok = pl.BlockSpec((None, slots, channels, width), lambda e: (e, 0, 0, 0))
    weight = pl.BlockSpec((None, channels, hidden), lambda e: (e, 0, 0))
    return pl.pallas_call(
        expert_kernel,
        grid=(experts,),
        out_shape=[
            jax.ShapeDtypeStruct(inputs.shape, jnp.bfloat16),
            jax.ShapeDtypeStruct((experts, 2, pieces, channels, 128), jnp.float32),
        ],
        in_specs=[tok, tok, weight, weight],
        out_specs=[tok, pl.BlockSpec((None, 2, pieces, channels, 128), lambda e: (e, 0, 0, 0, 0))],
        compiler_params=pltpu.CompilerParams(vmem_limit_bytes=48 * 1024 * 1024),
    )(inputs, grads, w_in, w_out_t)

def assemble_kernel(slot_ref, dense_ref, ret_ref, out_ref):
    per_row = dense_ref.shape[2] // ret_ref.shape[2]
    width = ret_ref.shape[2]
    for b in range(dense_ref.shape[0] * per_row):
        h, k = b // per_row, b % per_row
        piece = dense_ref[h, :, k * width:(k + 1) * width].astype(jnp.float32)
        piece = piece + ret_ref[slot_ref[b]].astype(jnp.float32)
        out_ref[h, :, k * width:(k + 1) * width] = piece.astype(out_ref.dtype)


def assemble(slot_of, dense_t, ret):
    return pl.pallas_call(
        assemble_kernel,
        out_shape=jax.ShapeDtypeStruct(dense_t.shape, dense_t.dtype),
        in_specs=[
            pl.BlockSpec(memory_space=pltpu.SMEM),
            pl.BlockSpec(memory_space=pltpu.VMEM),
            pl.BlockSpec(memory_space=pltpu.VMEM),
        ],
        out_specs=pl.BlockSpec(memory_space=pltpu.VMEM),
    )(slot_of, dense_t, ret)


def gelu_slope(values):
    return (
        0.5 * (1.0 + lax.erf(values * 0.7071067811865476))
        + values * jnp.exp(-0.5 * values * values) * 0.3989422804014327
    )


def depthwise(padded, kernel):
    row_count = padded.shape[1] - 6
    col_count = padded.shape[2] - 6
    summed = jnp.zeros((padded.shape[0], row_count, col_count, padded.shape[3]), jnp.float32)
    for row_off in range(7):
        for col_off in range(7):
            window = padded[:, row_off : row_off + row_count, col_off : col_off + col_count, :]
            summed = summed + window.astype(jnp.float32) * kernel[row_off, col_off]
    return summed


def widen(picture):
    return jnp.pad(picture, ((0, 0), (0, 0), (3, 3), (0, 0)))


def dense_block(images, smoothed, ln_gain, w_expand, w_reduce):
    channels = images.shape[-1]
    channel_mean = jnp.mean(smoothed, axis=-1, keepdims=True)
    centered = smoothed - channel_mean
    variance = jnp.mean(centered * centered, axis=-1, keepdims=True)
    normed = (centered * lax.rsqrt(variance + 1e-06) * ln_gain).astype(jnp.bfloat16)
    flat_normed = normed.reshape(-1, channels)
    expanded = jnp.dot(flat_normed, w_expand, preferred_element_type=jnp.float32)
    active = jax.nn.gelu(expanded, approximate=False).astype(jnp.bfloat16)
    reduced = jnp.dot(active, w_reduce, preferred_element_type=jnp.float32)
    dense_out = images.reshape(-1, channels).astype(jnp.float32) + reduced
    return dense_out.astype(jnp.bfloat16).reshape(images.shape)


def expert_pass(inputs, grads_in, w_in, w_out):
    pre_act = jnp.dot(inputs, w_in, preferred_element_type=jnp.float32)
    hidden = jax.nn.gelu(pre_act, approximate=False).astype(jnp.bfloat16)
    outputs = jnp.dot(hidden, w_out, preferred_element_type=jnp.float32).astype(jnp.bfloat16)
    grad_out = jnp.dot(hidden.T, grads_in, preferred_element_type=jnp.float32)
    back_prop = jnp.dot(grads_in, w_out.T, preferred_element_type=jnp.float32)
    scaled = (back_prop * gelu_slope(pre_act)).astype(jnp.bfloat16)
    grad_in = jnp.dot(inputs.T, scaled, preferred_element_type=jnp.float32)
    return (outputs, grad_in, grad_out)


def body(images, cotangent, labels, dw_kernel, ln_gain, w_expand, w_reduce, exp_in, exp_out):
    channels = images.shape[-1]
    padded = with_halo(images, (("lat", 1),), 3)
    smoothed = depthwise(widen(padded), dw_kernel)
    dense_out = dense_block(images, smoothed, ln_gain, w_expand, w_reduce)
    rows, width = images.shape[1], images.shape[2]
    per_row = width // BLOCK

    def to_blocks(pixels):
        pixels = pixels.reshape(rows, per_row, BLOCK, channels)
        return jnp.transpose(pixels, (0, 1, 3, 2)).reshape(rows * per_row, channels, BLOCK)

    blocks = to_blocks(dense_out)
    grad_blocks = to_blocks(cotangent)
    flat_labels = labels.reshape(-1)
    members = (flat_labels[:, None] == jnp.arange(EXPERTS, dtype=jnp.int32)[None, :]).astype(
        jnp.int32
    )
    before = jnp.sum(jnp.cumsum(members, axis=0) * members, axis=1) - 1
    slot_of = flat_labels * CAP + before
    placer = jnp.arange(EXPERTS * CAP, dtype=jnp.int32)[:, None] == slot_of[None, :]
    block_of_slot = jnp.argmax(placer, axis=1)
    filled = jnp.any(placer, axis=1)[:, None, None]
    outgoing = blocks[block_of_slot].reshape(EXPERTS, CAP, channels, BLOCK)
    outgoing_grads = jnp.where(filled, grad_blocks[block_of_slot], jnp.zeros((), jnp.bfloat16)).reshape(
        EXPERTS, CAP, channels, BLOCK
    )
    arrived, arrived_grads = (
        lax.all_to_all(outgoing, "exp", split_axis=0, concat_axis=1, tiled=True),
        lax.all_to_all(outgoing_grads, "exp", split_axis=0, concat_axis=1, tiled=True),
    )
    local = arrived.shape[0]
    results, flat = run_experts(arrived, arrived_grads, exp_in, jnp.transpose(exp_out, (0, 2, 1)))
    returned = lax.all_to_all(results, "exp", split_axis=1, concat_axis=0, tiled=True)
    grad_in, grad_out_t = tree_allreduce(flat.reshape(-1, 128), local, channels, exp_in.shape[2])
    grad_out = jnp.transpose(grad_out_t, (0, 2, 1))
    dense_t = jnp.transpose(dense_out.reshape(rows, width, channels), (0, 2, 1))
    out_t = assemble(slot_of.astype(jnp.int32), dense_t, returned.reshape(EXPERTS * CAP, channels, BLOCK))
    output = jnp.transpose(out_t, (0, 2, 1)).reshape(dense_out.shape)
    return (output, grad_in, grad_out)


def solution(mesh):
    in_specs = (
        P(("dp", "exp"), "lat", None, None),
        P(("dp", "exp"), "lat", None, None),
        P(("dp", "exp"), "lat", None, None),
        P(),
        P(),
        P(),
        P(),
        P("exp", None, None),
        P("exp", None, None),
    )
    out_specs = (P(("dp", "exp"), "lat", None, None), P("exp", None, None), P("exp", None, None))
    return jax.shard_map(body, mesh=mesh, in_specs=in_specs, out_specs=out_specs, check_vma=False)
```

```python
import jax
import jax.numpy as jnp
from jax import lax
from jax.sharding import PartitionSpec as P
from jax.experimental import pallas as pl
from jax.experimental.pallas import tpu as pltpu

EXPERTS = 16
BLOCK = 128
CAP = 3


def with_halo(block, sides, width):
    for axis, dim in sides:
        count = lax.axis_size(axis)
        forward = [(i, i + 1) for i in range(count - 1)]
        backward = [(target, source) for source, target in forward]
        low = lax.ppermute(
            lax.slice_in_dim(block, block.shape[dim] - width, None, axis=dim), axis, forward
        )
        high = lax.ppermute(lax.slice_in_dim(block, 0, width, axis=dim), axis, backward)
        block = jnp.concatenate([low, block, high], axis=dim)
    return block


def reduce_plan(lat_size, dp_size):
    dp_bits = dp_size.bit_length() - 1
    rest = list(range(1, dp_bits))
    other = rest[2:] + rest[:2] if len(rest) > 2 else rest
    plan = [("dp", 0, 0)] + [("dp", a, b) for a, b in zip(rest, other)]
    plan += [("lat", 0, 0)] * (lat_size.bit_length() - 1)
    return plan


def allreduce_kernel(plan, rows, in_ref, out_in, out_outt, *scratch):
    stages = len(plan)
    bufs = scratch[:stages]
    sums = scratch[stages:2 * stages]
    staged = scratch[2 * stages:3 * stages]
    gathered = scratch[3 * stages]
    rs_send, rs_recv, ag_send, ag_recv = scratch[3 * stages + 1:]
    lat = lax.axis_index("lat")
    dp = lax.axis_index("dp")
    ex = lax.axis_index("exp")
    core = dp % 2

    bits, partners = [], []
    for axis, b0, b1 in plan:
        me = dp if axis == "dp" else lat
        bit = jnp.where(core == 0, (me // (1 << b0)) % 2, (me // (1 << b1)) % 2)
        step = jnp.where(core == 0, 1 << b0, 1 << b1)
        other = me + (1 - 2 * bit) * step
        bits.append(bit)
        partners.append((lat, other, ex) if axis == "dp" else (other, dp, ex))

    barrier = pltpu.get_barrier_semaphore()
    for dev in partners:
        pl.semaphore_signal(barrier, 1, device_id=dev, device_id_type=pl.DeviceIdType.MESH)
    pl.semaphore_wait(barrier, stages)

    def chunked(count, body):
        chunk = min(count, 1152)
        lax.fori_loop(0, count // chunk, lambda i, c: (body(pl.multiple_of(i * chunk, 16), chunk), c)[1], 0)

    los = []
    lo = jnp.int32(0)
    for k in range(stages):
        half = rows >> (k + 1)
        los.append(lo)
        src = in_ref if k == 0 else sums[k - 1]
        keep = bits[k] * half
        give = (1 - bits[k]) * half

        def narrow(at, chunk, src=src, give=give, k=k):
            staged[k][pl.ds(at, chunk)] = src[pl.ds(pl.multiple_of(give + at, 16), chunk)].astype(jnp.bfloat16)

        def add(at, chunk, src=src, keep=keep, k=k):
            sums[k][pl.ds(at, chunk)] = src[pl.ds(pl.multiple_of(keep + at, 16), chunk)] + bufs[k][
                pl.ds(at, chunk)
            ].astype(jnp.float32)

        parts = 2 if half >= 576 else 1
        piece = half // parts
        copies = []
        for p in range(parts):
            lax.fori_loop(
                0,
                piece // min(piece, 1152),
                lambda i, c, p=p, narrow=narrow: (
                    narrow(pl.multiple_of(p * piece + i * min(piece, 1152), 16), min(piece, 1152)),
                    c,
                )[1],
                0,
            )
            copy = pltpu.make_async_remote_copy(
                src_ref=staged[k].at[pl.ds(p * piece, piece)],
                dst_ref=bufs[k].at[pl.ds(p * piece, piece)],
                send_sem=rs_send.at[2 * k + p],
                recv_sem=rs_recv.at[2 * k + p],
                device_id=partners[k],
                device_id_type=pl.DeviceIdType.MESH,
            )
            copy.start()
            copies.append(copy)
        for p in range(parts):
            copies[p].wait()
            lax.fori_loop(
                0,
                piece // min(piece, 1152),
                lambda i, c, p=p, add=add: (
                    add(pl.multiple_of(p * piece + i * min(piece, 1152), 16), min(piece, 1152)),
                    c,
                )[1],
                0,
            )
        lo = lo + bits[k] * half

    last = rows >> stages
    lo = pl.multiple_of(lo, 16)
    gathered[pl.ds(lo, last)] = sums[stages - 1][...].astype(jnp.bfloat16)
    for k in reversed(range(stages)):
        half = rows >> (k + 1)
        copy = pltpu.make_async_remote_copy(
            src_ref=gathered.at[pl.ds(pl.multiple_of(lo, 16), half)],
            dst_ref=gathered.at[pl.ds(pl.multiple_of(lo, 16), half)],
            send_sem=ag_send.at[k],
            recv_sem=ag_recv.at[k],
            device_id=partners[k],
            device_id_type=pl.DeviceIdType.MESH,
        )
        copy.start()
        copy.wait()
        lo = los[k]

    experts, channels, hidden = out_in.shape
    pieces = hidden // 128
    for e in range(experts):
        for t, dst in enumerate((out_in, out_outt)):
            for c in range(pieces):
                at = ((e * 2 + t) * pieces + c) * channels
                dst[e, :, c * 128:(c + 1) * 128] = gathered[at:at + channels].astype(jnp.float32)


def tree_allreduce(flat, experts, channels, hidden):
    rows = flat.shape[0]
    plan = reduce_plan(lax.axis_size("lat"), lax.axis_size("dp"))
    stages = len(plan)
    scratch = [pltpu.VMEM((rows >> (k + 1), 128), jnp.bfloat16) for k in range(stages)]
    scratch += [pltpu.VMEM((rows >> (k + 1), 128), jnp.float32) for k in range(stages)]
    scratch += [pltpu.VMEM((rows >> (k + 1), 128), jnp.bfloat16) for k in range(stages)]
    scratch += [pltpu.VMEM((rows, 128), jnp.bfloat16)]
    scratch += [pltpu.SemaphoreType.DMA((2 * stages,))] * 2 + [pltpu.SemaphoreType.DMA((stages,))] * 2
    return pl.pallas_call(
        lambda *refs: allreduce_kernel(plan, rows, *refs),
        out_shape=[jax.ShapeDtypeStruct((experts, channels, hidden), jnp.float32)] * 2,
        in_specs=[pl.BlockSpec(memory_space=pltpu.VMEM)],
        out_specs=[pl.BlockSpec(memory_space=pltpu.VMEM)] * 2,
        scratch_shapes=scratch,
        compiler_params=pltpu.CompilerParams(
            collective_id=0, has_side_effects=True, vmem_limit_bytes=62 * 1024 * 1024
        ),
    )(flat)

def expert_kernel(x_ref, g_ref, win_ref, wout_ref, out_ref, flat_ref):
    slots = x_ref.shape[0]
    x_t = jnp.concatenate([x_ref[s] for s in range(slots)], axis=1)
    g_t = jnp.concatenate([g_ref[s] for s in range(slots)], axis=1)
    w_out_t = wout_ref[...]
    pre = lax.dot_general(x_t, win_ref[...], (((0,), (0,)), ((), ())), preferred_element_type=jnp.float32)
    cdf = 0.5 * (1.0 + lax.erf(pre * 0.7071067811865476))
    hidden = (pre * cdf).astype(jnp.bfloat16)
    out_t = lax.dot_general(w_out_t, hidden, (((1,), (1,)), ((), ())), preferred_element_type=jnp.float32)
    out_t = out_t.astype(out_ref.dtype)
    width = out_ref.shape[2]
    for s in range(slots):
        out_ref[s] = out_t[:, s * width:(s + 1) * width]
    grad_out_t = jnp.dot(g_t, hidden, preferred_element_type=jnp.float32)
    back = lax.dot_general(g_t, w_out_t, (((0,), (0,)), ((), ())), preferred_element_type=jnp.float32)
    slope = cdf + pre * jnp.exp(-0.5 * pre * pre) * 0.3989422804014327
    scaled = (back * slope).astype(jnp.bfloat16)
    grad_in = jnp.dot(x_t, scaled, preferred_element_type=jnp.float32)
    for c in range(grad_in.shape[1] // 128):
        flat_ref[0, c] = grad_in[:, c * 128:(c + 1) * 128]
        flat_ref[1, c] = grad_out_t[:, c * 128:(c + 1) * 128]


def run_experts(inputs, grads, w_in, w_out_t):
    experts, slots, channels, width = inputs.shape
    hidden = w_in.shape[2]
    pieces = hidden // 128
    tok = pl.BlockSpec((None, slots, channels, width), lambda e: (e, 0, 0, 0))
    weight = pl.BlockSpec((None, channels, hidden), lambda e: (e, 0, 0))
    return pl.pallas_call(
        expert_kernel,
        grid=(experts,),
        out_shape=[
            jax.ShapeDtypeStruct(inputs.shape, jnp.bfloat16),
            jax.ShapeDtypeStruct((experts, 2, pieces, channels, 128), jnp.float32),
        ],
        in_specs=[tok, tok, weight, weight],
        out_specs=[tok, pl.BlockSpec((None, 2, pieces, channels, 128), lambda e: (e, 0, 0, 0, 0))],
        compiler_params=pltpu.CompilerParams(vmem_limit_bytes=48 * 1024 * 1024),
    )(inputs, grads, w_in, w_out_t)

def assemble_kernel(slot_ref, dense_ref, ret_ref, out_ref):
    per_row = dense_ref.shape[2] // ret_ref.shape[2]
    width = ret_ref.shape[2]
    for b in range(dense_ref.shape[0] * per_row):
        h, k = b // per_row, b % per_row
        piece = dense_ref[h, :, k * width:(k + 1) * width].astype(jnp.float32)
        piece = piece + ret_ref[slot_ref[b]].astype(jnp.float32)
        out_ref[h, :, k * width:(k + 1) * width] = piece.astype(out_ref.dtype)


def assemble(slot_of, dense_t, ret):
    return pl.pallas_call(
        assemble_kernel,
        out_shape=jax.ShapeDtypeStruct(dense_t.shape, dense_t.dtype),
        in_specs=[
            pl.BlockSpec(memory_space=pltpu.SMEM),
            pl.BlockSpec(memory_space=pltpu.VMEM),
            pl.BlockSpec(memory_space=pltpu.VMEM),
        ],
        out_specs=pl.BlockSpec(memory_space=pltpu.VMEM),
    )(slot_of, dense_t, ret)


def place_kernel(source_ref, filled_ref, src_ref, out_ref):
    width = out_ref.shape[2]
    per_row = src_ref.shape[2] // width
    for s in range(out_ref.shape[0]):
        b = source_ref[s]
        row = src_ref[b // per_row]
        k = b % per_row
        piece = row[:, 0:width]
        for j in range(1, per_row):
            piece = jnp.where(k == j, row[:, j * width:(j + 1) * width], piece)
        out_ref[s] = jnp.where(filled_ref[s] > 0, piece, jnp.zeros_like(piece))


def place(block_of_slot, filled, src_t, width):
    slots = block_of_slot.shape[0]
    return pl.pallas_call(
        place_kernel,
        out_shape=jax.ShapeDtypeStruct((slots, src_t.shape[1], width), src_t.dtype),
        in_specs=[
            pl.BlockSpec(memory_space=pltpu.SMEM),
            pl.BlockSpec(memory_space=pltpu.SMEM),
            pl.BlockSpec(memory_space=pltpu.VMEM),
        ],
        out_specs=pl.BlockSpec(memory_space=pltpu.VMEM),
    )(block_of_slot, filled, src_t)


def gelu_slope(values):
    return (
        0.5 * (1.0 + lax.erf(values * 0.7071067811865476))
        + values * jnp.exp(-0.5 * values * values) * 0.3989422804014327
    )


def depthwise(padded, kernel):
    row_count = padded.shape[1] - 6
    col_count = padded.shape[2] - 6
    summed = jnp.zeros((padded.shape[0], row_count, col_count, padded.shape[3]), jnp.float32)
    for row_off in range(7):
        for col_off in range(7):
            window = padded[:, row_off : row_off + row_count, col_off : col_off + col_count, :]
            summed = summed + window.astype(jnp.float32) * kernel[row_off, col_off]
    return summed


def widen(picture):
    return jnp.pad(picture, ((0, 0), (0, 0), (3, 3), (0, 0)))


def dense_block(images, smoothed, ln_gain, w_expand, w_reduce):
    channels = images.shape[-1]
    channel_mean = jnp.mean(smoothed, axis=-1, keepdims=True)
    centered = smoothed - channel_mean
    variance = jnp.mean(centered * centered, axis=-1, keepdims=True)
    normed = (centered * lax.rsqrt(variance + 1e-06) * ln_gain).astype(jnp.bfloat16)
    flat_normed = normed.reshape(-1, channels)
    expanded = jnp.dot(flat_normed, w_expand, preferred_element_type=jnp.float32)
    active = jax.nn.gelu(expanded, approximate=False).astype(jnp.bfloat16)
    reduced = jnp.dot(active, w_reduce, preferred_element_type=jnp.float32)
    dense_out = images.reshape(-1, channels).astype(jnp.float32) + reduced
    return dense_out.astype(jnp.bfloat16).reshape(images.shape)


def expert_pass(inputs, grads_in, w_in, w_out):
    pre_act = jnp.dot(inputs, w_in, preferred_element_type=jnp.float32)
    hidden = jax.nn.gelu(pre_act, approximate=False).astype(jnp.bfloat16)
    outputs = jnp.dot(hidden, w_out, preferred_element_type=jnp.float32).astype(jnp.bfloat16)
    grad_out = jnp.dot(hidden.T, grads_in, preferred_element_type=jnp.float32)
    back_prop = jnp.dot(grads_in, w_out.T, preferred_element_type=jnp.float32)
    scaled = (back_prop * gelu_slope(pre_act)).astype(jnp.bfloat16)
    grad_in = jnp.dot(inputs.T, scaled, preferred_element_type=jnp.float32)
    return (outputs, grad_in, grad_out)


def body(images, cotangent, labels, dw_kernel, ln_gain, w_expand, w_reduce, exp_in, exp_out):
    channels = images.shape[-1]
    padded = with_halo(images, (("lat", 1),), 3)
    smoothed = depthwise(widen(padded), dw_kernel)
    dense_out = dense_block(images, smoothed, ln_gain, w_expand, w_reduce)
    rows, width = images.shape[1], images.shape[2]
    per_row = width // BLOCK

    def to_blocks(pixels):
        pixels = pixels.reshape(rows, per_row, BLOCK, channels)
        return jnp.transpose(pixels, (0, 1, 3, 2)).reshape(rows * per_row, channels, BLOCK)

    flat_labels = labels.reshape(-1)
    members = (flat_labels[:, None] == jnp.arange(EXPERTS, dtype=jnp.int32)[None, :]).astype(
        jnp.int32
    )
    before = jnp.sum(jnp.cumsum(members, axis=0) * members, axis=1) - 1
    slot_of = flat_labels * CAP + before
    placer = jnp.arange(EXPERTS * CAP, dtype=jnp.int32)[:, None] == slot_of[None, :]
    block_of_slot = jnp.argmax(placer, axis=1)
    filled = jnp.any(placer, axis=1)[:, None, None]
    source = block_of_slot.astype(jnp.int32)
    flags = filled.reshape(-1).astype(jnp.int32)
    keep_all = jnp.ones_like(flags)
    dense_t = jnp.transpose(dense_out.reshape(rows, width, channels), (0, 2, 1))
    cot_t = jnp.transpose(cotangent.reshape(rows, width, channels), (0, 2, 1))
    outgoing = place(source, keep_all, dense_t, BLOCK).reshape(EXPERTS, CAP, channels, BLOCK)
    outgoing_grads = place(source, flags, cot_t, BLOCK).reshape(EXPERTS, CAP, channels, BLOCK)
    arrived, arrived_grads = (
        lax.all_to_all(outgoing, "exp", split_axis=0, concat_axis=1, tiled=True),
        lax.all_to_all(outgoing_grads, "exp", split_axis=0, concat_axis=1, tiled=True),
    )
    local = arrived.shape[0]
    results, flat = run_experts(arrived, arrived_grads, exp_in, jnp.transpose(exp_out, (0, 2, 1)))
    returned = lax.all_to_all(results, "exp", split_axis=1, concat_axis=0, tiled=True)
    grad_in, grad_out_t = tree_allreduce(flat.reshape(-1, 128), local, channels, exp_in.shape[2])
    grad_out = jnp.transpose(grad_out_t, (0, 2, 1))
    out_t = assemble(slot_of.astype(jnp.int32), dense_t, returned.reshape(EXPERTS * CAP, channels, BLOCK))
    output = jnp.transpose(out_t, (0, 2, 1)).reshape(dense_out.shape)
    return (output, grad_in, grad_out)


def solution(mesh):
    in_specs = (
        P(("dp", "exp"), "lat", None, None),
        P(("dp", "exp"), "lat", None, None),
        P(("dp", "exp"), "lat", None, None),
        P(),
        P(),
        P(),
        P(),
        P("exp", None, None),
        P("exp", None, None),
    )
    out_specs = (P(("dp", "exp"), "lat", None, None), P("exp", None, None), P("exp", None, None))
    return jax.shard_map(body, mesh=mesh, in_specs=in_specs, out_specs=out_specs, check_vma=False)
```

```python
import jax
import jax.numpy as jnp
from jax import lax
from jax.sharding import PartitionSpec as P
from jax.experimental import pallas as pl
from jax.experimental.pallas import tpu as pltpu

EXPERTS = 16
BLOCK = 128
CAP = 3


def with_halo(block, sides, width):
    for axis, dim in sides:
        count = lax.axis_size(axis)
        forward = [(i, i + 1) for i in range(count - 1)]
        backward = [(target, source) for source, target in forward]
        low = lax.ppermute(
            lax.slice_in_dim(block, block.shape[dim] - width, None, axis=dim), axis, forward
        )
        high = lax.ppermute(lax.slice_in_dim(block, 0, width, axis=dim), axis, backward)
        block = jnp.concatenate([low, block, high], axis=dim)
    return block


def reduce_plan(lat_size, dp_size):
    dp_bits = dp_size.bit_length() - 1
    rest = list(range(1, dp_bits))
    other = rest[2:] + rest[:2] if len(rest) > 2 else rest
    plan = [("dp", 0, 0)] + [("dp", a, b) for a, b in zip(rest, other)]
    plan += [("lat", 0, 0)] * (lat_size.bit_length() - 1)
    return plan


def allreduce_kernel(plan, rows, in_ref, out_in, out_outt, *scratch):
    stages = len(plan)
    bufs = scratch[:stages]
    sums = scratch[stages:2 * stages]
    staged = scratch[2 * stages:3 * stages]
    gathered = scratch[3 * stages]
    rs_send, rs_recv, ag_send, ag_recv = scratch[3 * stages + 1:]
    lat = lax.axis_index("lat")
    dp = lax.axis_index("dp")
    ex = lax.axis_index("exp")
    core = dp % 2

    bits, partners = [], []
    for axis, b0, b1 in plan:
        me = dp if axis == "dp" else lat
        bit = jnp.where(core == 0, (me // (1 << b0)) % 2, (me // (1 << b1)) % 2)
        step = jnp.where(core == 0, 1 << b0, 1 << b1)
        other = me + (1 - 2 * bit) * step
        bits.append(bit)
        partners.append((lat, other, ex) if axis == "dp" else (other, dp, ex))

    barrier = pltpu.get_barrier_semaphore()
    for dev in partners:
        pl.semaphore_signal(barrier, 1, device_id=dev, device_id_type=pl.DeviceIdType.MESH)
    pl.semaphore_wait(barrier, stages)

    def chunked(count, body):
        chunk = min(count, 1152)
        lax.fori_loop(0, count // chunk, lambda i, c: (body(pl.multiple_of(i * chunk, 16), chunk), c)[1], 0)

    los = []
    lo = jnp.int32(0)
    for k in range(stages):
        half = rows >> (k + 1)
        los.append(lo)
        src = in_ref if k == 0 else sums[k - 1]
        keep = bits[k] * half
        give = (1 - bits[k]) * half

        def narrow(at, chunk, src=src, give=give, k=k):
            staged[k][pl.ds(at, chunk)] = src[pl.ds(pl.multiple_of(give + at, 16), chunk)].astype(jnp.bfloat16)

        def add(at, chunk, src=src, keep=keep, k=k):
            sums[k][pl.ds(at, chunk)] = src[pl.ds(pl.multiple_of(keep + at, 16), chunk)] + bufs[k][
                pl.ds(at, chunk)
            ].astype(jnp.float32)

        parts = 2 if half >= 576 else 1
        piece = half // parts
        copies = []
        for p in range(parts):
            lax.fori_loop(
                0,
                piece // min(piece, 1152),
                lambda i, c, p=p, narrow=narrow: (
                    narrow(pl.multiple_of(p * piece + i * min(piece, 1152), 16), min(piece, 1152)),
                    c,
                )[1],
                0,
            )
            copy = pltpu.make_async_remote_copy(
                src_ref=staged[k].at[pl.ds(p * piece, piece)],
                dst_ref=bufs[k].at[pl.ds(p * piece, piece)],
                send_sem=rs_send.at[2 * k + p],
                recv_sem=rs_recv.at[2 * k + p],
                device_id=partners[k],
                device_id_type=pl.DeviceIdType.MESH,
            )
            copy.start()
            copies.append(copy)
        for p in range(parts):
            copies[p].wait()
            lax.fori_loop(
                0,
                piece // min(piece, 1152),
                lambda i, c, p=p, add=add: (
                    add(pl.multiple_of(p * piece + i * min(piece, 1152), 16), min(piece, 1152)),
                    c,
                )[1],
                0,
            )
        lo = lo + bits[k] * half

    last = rows >> stages
    lo = pl.multiple_of(lo, 16)
    gathered[pl.ds(lo, last)] = sums[stages - 1][...].astype(jnp.bfloat16)
    for k in reversed(range(stages)):
        half = rows >> (k + 1)
        copy = pltpu.make_async_remote_copy(
            src_ref=gathered.at[pl.ds(pl.multiple_of(lo, 16), half)],
            dst_ref=gathered.at[pl.ds(pl.multiple_of(lo, 16), half)],
            send_sem=ag_send.at[k],
            recv_sem=ag_recv.at[k],
            device_id=partners[k],
            device_id_type=pl.DeviceIdType.MESH,
        )
        copy.start()
        copy.wait()
        lo = los[k]

    experts, channels, hidden = out_in.shape
    pieces = hidden // 128
    for e in range(experts):
        for t, dst in enumerate((out_in, out_outt)):
            for c in range(pieces):
                at = ((e * 2 + t) * pieces + c) * channels
                dst[e, :, c * 128:(c + 1) * 128] = gathered[at:at + channels].astype(jnp.float32)


def tree_allreduce(flat, experts, channels, hidden):
    rows = flat.shape[0]
    plan = reduce_plan(lax.axis_size("lat"), lax.axis_size("dp"))
    stages = len(plan)
    scratch = [pltpu.VMEM((rows >> (k + 1), 128), jnp.bfloat16) for k in range(stages)]
    scratch += [pltpu.VMEM((rows >> (k + 1), 128), jnp.float32) for k in range(stages)]
    scratch += [pltpu.VMEM((rows >> (k + 1), 128), jnp.bfloat16) for k in range(stages)]
    scratch += [pltpu.VMEM((rows, 128), jnp.bfloat16)]
    scratch += [pltpu.SemaphoreType.DMA((2 * stages,))] * 2 + [pltpu.SemaphoreType.DMA((stages,))] * 2
    return pl.pallas_call(
        lambda *refs: allreduce_kernel(plan, rows, *refs),
        out_shape=[jax.ShapeDtypeStruct((experts, channels, hidden), jnp.float32)] * 2,
        in_specs=[pl.BlockSpec(memory_space=pltpu.VMEM)],
        out_specs=[pl.BlockSpec(memory_space=pltpu.VMEM)] * 2,
        scratch_shapes=scratch,
        compiler_params=pltpu.CompilerParams(
            collective_id=0, has_side_effects=True, vmem_limit_bytes=62 * 1024 * 1024
        ),
    )(flat)

def expert_kernel(x_ref, g_ref, win_ref, wout_ref, out_ref, flat_ref):
    sources, per_source = x_ref.shape[0], x_ref.shape[1]
    slots = sources * per_source
    x_t = jnp.concatenate([x_ref[s // per_source, s % per_source] for s in range(slots)], axis=1)
    g_t = jnp.concatenate([g_ref[s // per_source, s % per_source] for s in range(slots)], axis=1)
    w_out_t = wout_ref[...]
    pre = lax.dot_general(x_t, win_ref[...], (((0,), (0,)), ((), ())), preferred_element_type=jnp.float32)
    cdf = 0.5 * (1.0 + lax.erf(pre * 0.7071067811865476))
    hidden = (pre * cdf).astype(jnp.bfloat16)
    out_t = lax.dot_general(w_out_t, hidden, (((1,), (1,)), ((), ())), preferred_element_type=jnp.float32)
    out_t = out_t.astype(out_ref.dtype)
    width = out_ref.shape[3]
    for s in range(slots):
        out_ref[s // per_source, s % per_source] = out_t[:, s * width:(s + 1) * width]
    grad_out_t = jnp.dot(g_t, hidden, preferred_element_type=jnp.float32)
    back = lax.dot_general(g_t, w_out_t, (((0,), (0,)), ((), ())), preferred_element_type=jnp.float32)
    slope = cdf + pre * jnp.exp(-0.5 * pre * pre) * 0.3989422804014327
    scaled = (back * slope).astype(jnp.bfloat16)
    grad_in = jnp.dot(x_t, scaled, preferred_element_type=jnp.float32)
    for c in range(grad_in.shape[1] // 128):
        flat_ref[0, c] = grad_in[:, c * 128:(c + 1) * 128]
        flat_ref[1, c] = grad_out_t[:, c * 128:(c + 1) * 128]


def run_experts(inputs, grads, w_in, w_out_t):
    sources, experts, per_source, channels, width = inputs.shape
    hidden = w_in.shape[2]
    pieces = hidden // 128
    tok = pl.BlockSpec((sources, None, per_source, channels, width), lambda e: (0, e, 0, 0, 0))
    weight = pl.BlockSpec((None, channels, hidden), lambda e: (e, 0, 0))
    return pl.pallas_call(
        expert_kernel,
        grid=(experts,),
        out_shape=[
            jax.ShapeDtypeStruct(inputs.shape, jnp.bfloat16),
            jax.ShapeDtypeStruct((experts, 2, pieces, channels, 128), jnp.float32),
        ],
        in_specs=[tok, tok, weight, weight],
        out_specs=[tok, pl.BlockSpec((None, 2, pieces, channels, 128), lambda e: (e, 0, 0, 0, 0))],
        compiler_params=pltpu.CompilerParams(vmem_limit_bytes=48 * 1024 * 1024),
    )(inputs, grads, w_in, w_out_t)

def assemble_kernel(slot_ref, dense_ref, ret_ref, out_ref):
    per_row = dense_ref.shape[2] // ret_ref.shape[2]
    width = ret_ref.shape[2]
    for b in range(dense_ref.shape[0] * per_row):
        h, k = b // per_row, b % per_row
        piece = dense_ref[h, :, k * width:(k + 1) * width].astype(jnp.float32)
        piece = piece + ret_ref[slot_ref[b]].astype(jnp.float32)
        out_ref[h, :, k * width:(k + 1) * width] = piece.astype(out_ref.dtype)


def assemble(slot_of, dense_t, ret):
    return pl.pallas_call(
        assemble_kernel,
        out_shape=jax.ShapeDtypeStruct(dense_t.shape, dense_t.dtype),
        in_specs=[
            pl.BlockSpec(memory_space=pltpu.SMEM),
            pl.BlockSpec(memory_space=pltpu.VMEM),
            pl.BlockSpec(memory_space=pltpu.VMEM),
        ],
        out_specs=pl.BlockSpec(memory_space=pltpu.VMEM),
    )(slot_of, dense_t, ret)


def place_kernel(source_ref, filled_ref, src_ref, out_ref):
    width = out_ref.shape[2]
    per_row = src_ref.shape[2] // width
    for s in range(out_ref.shape[0]):
        b = source_ref[s]
        row = src_ref[b // per_row]
        k = b % per_row
        piece = row[:, 0:width]
        for j in range(1, per_row):
            piece = jnp.where(k == j, row[:, j * width:(j + 1) * width], piece)
        out_ref[s] = jnp.where(filled_ref[s] > 0, piece, jnp.zeros_like(piece))


def place(block_of_slot, filled, src_t, width):
    slots = block_of_slot.shape[0]
    return pl.pallas_call(
        place_kernel,
        out_shape=jax.ShapeDtypeStruct((slots, src_t.shape[1], width), src_t.dtype),
        in_specs=[
            pl.BlockSpec(memory_space=pltpu.SMEM),
            pl.BlockSpec(memory_space=pltpu.SMEM),
            pl.BlockSpec(memory_space=pltpu.VMEM),
        ],
        out_specs=pl.BlockSpec(memory_space=pltpu.VMEM),
    )(block_of_slot, filled, src_t)


def gelu_slope(values):
    return (
        0.5 * (1.0 + lax.erf(values * 0.7071067811865476))
        + values * jnp.exp(-0.5 * values * values) * 0.3989422804014327
    )


def depthwise(padded, kernel):
    row_count = padded.shape[1] - 6
    col_count = padded.shape[2] - 6
    summed = jnp.zeros((padded.shape[0], row_count, col_count, padded.shape[3]), jnp.float32)
    for row_off in range(7):
        for col_off in range(7):
            window = padded[:, row_off : row_off + row_count, col_off : col_off + col_count, :]
            summed = summed + window.astype(jnp.float32) * kernel[row_off, col_off]
    return summed


def widen(picture):
    return jnp.pad(picture, ((0, 0), (0, 0), (3, 3), (0, 0)))


def dense_block(images, smoothed, ln_gain, w_expand, w_reduce):
    channels = images.shape[-1]
    channel_mean = jnp.mean(smoothed, axis=-1, keepdims=True)
    centered = smoothed - channel_mean
    variance = jnp.mean(centered * centered, axis=-1, keepdims=True)
    normed = (centered * lax.rsqrt(variance + 1e-06) * ln_gain).astype(jnp.bfloat16)
    flat_normed = normed.reshape(-1, channels)
    expanded = jnp.dot(flat_normed, w_expand, preferred_element_type=jnp.float32)
    active = jax.nn.gelu(expanded, approximate=False).astype(jnp.bfloat16)
    reduced = jnp.dot(active, w_reduce, preferred_element_type=jnp.float32)
    dense_out = images.reshape(-1, channels).astype(jnp.float32) + reduced
    return dense_out.astype(jnp.bfloat16).reshape(images.shape)


def expert_pass(inputs, grads_in, w_in, w_out):
    pre_act = jnp.dot(inputs, w_in, preferred_element_type=jnp.float32)
    hidden = jax.nn.gelu(pre_act, approximate=False).astype(jnp.bfloat16)
    outputs = jnp.dot(hidden, w_out, preferred_element_type=jnp.float32).astype(jnp.bfloat16)
    grad_out = jnp.dot(hidden.T, grads_in, preferred_element_type=jnp.float32)
    back_prop = jnp.dot(grads_in, w_out.T, preferred_element_type=jnp.float32)
    scaled = (back_prop * gelu_slope(pre_act)).astype(jnp.bfloat16)
    grad_in = jnp.dot(inputs.T, scaled, preferred_element_type=jnp.float32)
    return (outputs, grad_in, grad_out)


def body(images, cotangent, labels, dw_kernel, ln_gain, w_expand, w_reduce, exp_in, exp_out):
    channels = images.shape[-1]
    padded = with_halo(images, (("lat", 1),), 3)
    smoothed = depthwise(widen(padded), dw_kernel)
    dense_out = dense_block(images, smoothed, ln_gain, w_expand, w_reduce)
    rows, width = images.shape[1], images.shape[2]
    per_row = width // BLOCK

    def to_blocks(pixels):
        pixels = pixels.reshape(rows, per_row, BLOCK, channels)
        return jnp.transpose(pixels, (0, 1, 3, 2)).reshape(rows * per_row, channels, BLOCK)

    flat_labels = labels.reshape(-1)
    members = (flat_labels[:, None] == jnp.arange(EXPERTS, dtype=jnp.int32)[None, :]).astype(
        jnp.int32
    )
    before = jnp.sum(jnp.cumsum(members, axis=0) * members, axis=1) - 1
    slot_of = flat_labels * CAP + before
    placer = jnp.arange(EXPERTS * CAP, dtype=jnp.int32)[:, None] == slot_of[None, :]
    block_of_slot = jnp.argmax(placer, axis=1)
    filled = jnp.any(placer, axis=1)[:, None, None]
    source = block_of_slot.astype(jnp.int32)
    flags = filled.reshape(-1).astype(jnp.int32)
    keep_all = jnp.ones_like(flags)
    dense_t = jnp.transpose(dense_out.reshape(rows, width, channels), (0, 2, 1))
    cot_t = jnp.transpose(cotangent.reshape(rows, width, channels), (0, 2, 1))
    outgoing = place(source, keep_all, dense_t, BLOCK).reshape(EXPERTS, CAP, channels, BLOCK)
    outgoing_grads = place(source, flags, cot_t, BLOCK).reshape(EXPERTS, CAP, channels, BLOCK)
    groups = lax.axis_size("exp")
    local = EXPERTS // groups
    by_group = (groups, local, CAP, channels, BLOCK)
    arrived, arrived_grads = (
        lax.all_to_all(outgoing.reshape(by_group), "exp", split_axis=0, concat_axis=0, tiled=True),
        lax.all_to_all(outgoing_grads.reshape(by_group), "exp", split_axis=0, concat_axis=0, tiled=True),
    )
    results, flat = run_experts(arrived, arrived_grads, exp_in, jnp.transpose(exp_out, (0, 2, 1)))
    returned = lax.all_to_all(results, "exp", split_axis=0, concat_axis=0, tiled=True)
    grad_in, grad_out_t = tree_allreduce(flat.reshape(-1, 128), local, channels, exp_in.shape[2])
    grad_out = jnp.transpose(grad_out_t, (0, 2, 1))
    out_t = assemble(slot_of.astype(jnp.int32), dense_t, returned.reshape(EXPERTS * CAP, channels, BLOCK))
    output = jnp.transpose(out_t, (0, 2, 1)).reshape(dense_out.shape)
    return (output, grad_in, grad_out)


def solution(mesh):
    in_specs = (
        P(("dp", "exp"), "lat", None, None),
        P(("dp", "exp"), "lat", None, None),
        P(("dp", "exp"), "lat", None, None),
        P(),
        P(),
        P(),
        P(),
        P("exp", None, None),
        P("exp", None, None),
    )
    out_specs = (P(("dp", "exp"), "lat", None, None), P("exp", None, None), P("exp", None, None))
    return jax.shard_map(body, mesh=mesh, in_specs=in_specs, out_specs=out_specs, check_vma=False)
```

```python
import jax
import jax.numpy as jnp
from jax import lax
from jax.sharding import PartitionSpec as P
from jax.experimental import pallas as pl
from jax.experimental.pallas import tpu as pltpu

EXPERTS = 16
BLOCK = 128
CAP = 3


def with_halo(block, sides, width):
    for axis, dim in sides:
        count = lax.axis_size(axis)
        forward = [(i, i + 1) for i in range(count - 1)]
        backward = [(target, source) for source, target in forward]
        low = lax.ppermute(
            lax.slice_in_dim(block, block.shape[dim] - width, None, axis=dim), axis, forward
        )
        high = lax.ppermute(lax.slice_in_dim(block, 0, width, axis=dim), axis, backward)
        block = jnp.concatenate([low, block, high], axis=dim)
    return block


def reduce_plan(lat_size, dp_size):
    dp_bits = dp_size.bit_length() - 1
    rest = list(range(1, dp_bits))
    other = rest[2:] + rest[:2] if len(rest) > 2 else rest
    plan = [("dp", 0, 0)] + [("dp", a, b) for a, b in zip(rest, other)]
    plan += [("lat", 0, 0)] * (lat_size.bit_length() - 1)
    return plan


def allreduce_kernel(plan, rows, in_ref, out_in, out_outt, *scratch):
    stages = len(plan)
    bufs = scratch[:stages]
    sums = scratch[stages:2 * stages]
    staged = scratch[2 * stages:3 * stages]
    gathered = scratch[3 * stages]
    rs_send, rs_recv, ag_send, ag_recv = scratch[3 * stages + 1:]
    lat = lax.axis_index("lat")
    dp = lax.axis_index("dp")
    ex = lax.axis_index("exp")
    core = dp % 2

    bits, partners = [], []
    for axis, b0, b1 in plan:
        me = dp if axis == "dp" else lat
        bit = jnp.where(core == 0, (me // (1 << b0)) % 2, (me // (1 << b1)) % 2)
        step = jnp.where(core == 0, 1 << b0, 1 << b1)
        other = me + (1 - 2 * bit) * step
        bits.append(bit)
        partners.append((lat, other, ex) if axis == "dp" else (other, dp, ex))

    barrier = pltpu.get_barrier_semaphore()
    for dev in partners:
        pl.semaphore_signal(barrier, 1, device_id=dev, device_id_type=pl.DeviceIdType.MESH)
    pl.semaphore_wait(barrier, stages)

    def chunked(count, body):
        chunk = min(count, 1152)
        lax.fori_loop(0, count // chunk, lambda i, c: (body(pl.multiple_of(i * chunk, 16), chunk), c)[1], 0)

    los = []
    lo = jnp.int32(0)
    for k in range(stages):
        half = rows >> (k + 1)
        los.append(lo)
        src = in_ref if k == 0 else sums[k - 1]
        keep = bits[k] * half
        give = (1 - bits[k]) * half

        def narrow(at, chunk, src=src, give=give, k=k):
            staged[k][pl.ds(at, chunk)] = src[pl.ds(pl.multiple_of(give + at, 16), chunk)].astype(jnp.bfloat16)

        def add(at, chunk, src=src, keep=keep, k=k):
            sums[k][pl.ds(at, chunk)] = src[pl.ds(pl.multiple_of(keep + at, 16), chunk)] + bufs[k][
                pl.ds(at, chunk)
            ].astype(jnp.float32)

        parts = 4 if half >= 4608 else (2 if half >= 576 else 1)
        piece = half // parts
        copies = []
        for p in range(parts):
            lax.fori_loop(
                0,
                piece // min(piece, 1152),
                lambda i, c, p=p, narrow=narrow: (
                    narrow(pl.multiple_of(p * piece + i * min(piece, 1152), 16), min(piece, 1152)),
                    c,
                )[1],
                0,
            )
            copy = pltpu.make_async_remote_copy(
                src_ref=staged[k].at[pl.ds(p * piece, piece)],
                dst_ref=bufs[k].at[pl.ds(p * piece, piece)],
                send_sem=rs_send.at[4 * k + p],
                recv_sem=rs_recv.at[4 * k + p],
                device_id=partners[k],
                device_id_type=pl.DeviceIdType.MESH,
            )
            copy.start()
            copies.append(copy)
        for p in range(parts):
            copies[p].wait()
            lax.fori_loop(
                0,
                piece // min(piece, 1152),
                lambda i, c, p=p, add=add: (
                    add(pl.multiple_of(p * piece + i * min(piece, 1152), 16), min(piece, 1152)),
                    c,
                )[1],
                0,
            )
        lo = lo + bits[k] * half

    last = rows >> stages
    lo = pl.multiple_of(lo, 16)
    gathered[pl.ds(lo, last)] = sums[stages - 1][...].astype(jnp.bfloat16)
    for k in reversed(range(stages)):
        half = rows >> (k + 1)
        copy = pltpu.make_async_remote_copy(
            src_ref=gathered.at[pl.ds(pl.multiple_of(lo, 16), half)],
            dst_ref=gathered.at[pl.ds(pl.multiple_of(lo, 16), half)],
            send_sem=ag_send.at[k],
            recv_sem=ag_recv.at[k],
            device_id=partners[k],
            device_id_type=pl.DeviceIdType.MESH,
        )
        copy.start()
        copy.wait()
        lo = los[k]

    experts, channels, hidden = out_in.shape
    pieces = hidden // 128
    for e in range(experts):
        for t, dst in enumerate((out_in, out_outt)):
            for c in range(pieces):
                at = ((e * 2 + t) * pieces + c) * channels
                dst[e, :, c * 128:(c + 1) * 128] = gathered[at:at + channels].astype(jnp.float32)


def tree_allreduce(flat, experts, channels, hidden):
    rows = flat.shape[0]
    plan = reduce_plan(lax.axis_size("lat"), lax.axis_size("dp"))
    stages = len(plan)
    scratch = [pltpu.VMEM((rows >> (k + 1), 128), jnp.bfloat16) for k in range(stages)]
    scratch += [pltpu.VMEM((rows >> (k + 1), 128), jnp.float32) for k in range(stages)]
    scratch += [pltpu.VMEM((rows >> (k + 1), 128), jnp.bfloat16) for k in range(stages)]
    scratch += [pltpu.VMEM((rows, 128), jnp.bfloat16)]
    scratch += [pltpu.SemaphoreType.DMA((4 * stages,))] * 2 + [pltpu.SemaphoreType.DMA((stages,))] * 2
    return pl.pallas_call(
        lambda *refs: allreduce_kernel(plan, rows, *refs),
        out_shape=[jax.ShapeDtypeStruct((experts, channels, hidden), jnp.float32)] * 2,
        in_specs=[pl.BlockSpec(memory_space=pltpu.VMEM)],
        out_specs=[pl.BlockSpec(memory_space=pltpu.VMEM)] * 2,
        scratch_shapes=scratch,
        compiler_params=pltpu.CompilerParams(
            collective_id=0, has_side_effects=True, vmem_limit_bytes=62 * 1024 * 1024
        ),
    )(flat)

def expert_kernel(x_ref, g_ref, win_ref, wout_ref, out_ref, flat_ref):
    sources, per_source = x_ref.shape[0], x_ref.shape[1]
    slots = sources * per_source
    x_t = jnp.concatenate([x_ref[s // per_source, s % per_source] for s in range(slots)], axis=1)
    g_t = jnp.concatenate([g_ref[s // per_source, s % per_source] for s in range(slots)], axis=1)
    w_out_t = wout_ref[...]
    pre = lax.dot_general(x_t, win_ref[...], (((0,), (0,)), ((), ())), preferred_element_type=jnp.float32)
    cdf = 0.5 * (1.0 + lax.erf(pre * 0.7071067811865476))
    hidden = (pre * cdf).astype(jnp.bfloat16)
    out_t = lax.dot_general(w_out_t, hidden, (((1,), (1,)), ((), ())), preferred_element_type=jnp.float32)
    out_t = out_t.astype(out_ref.dtype)
    width = out_ref.shape[3]
    for s in range(slots):
        out_ref[s // per_source, s % per_source] = out_t[:, s * width:(s + 1) * width]
    grad_out_t = jnp.dot(g_t, hidden, preferred_element_type=jnp.float32)
    back = lax.dot_general(g_t, w_out_t, (((0,), (0,)), ((), ())), preferred_element_type=jnp.float32)
    slope = cdf + pre * jnp.exp(-0.5 * pre * pre) * 0.3989422804014327
    scaled = (back * slope).astype(jnp.bfloat16)
    grad_in = jnp.dot(x_t, scaled, preferred_element_type=jnp.float32)
    for c in range(grad_in.shape[1] // 128):
        flat_ref[0, c] = grad_in[:, c * 128:(c + 1) * 128]
        flat_ref[1, c] = grad_out_t[:, c * 128:(c + 1) * 128]


def run_experts(inputs, grads, w_in, w_out_t):
    sources, experts, per_source, channels, width = inputs.shape
    hidden = w_in.shape[2]
    pieces = hidden // 128
    tok = pl.BlockSpec((sources, None, per_source, channels, width), lambda e: (0, e, 0, 0, 0))
    weight = pl.BlockSpec((None, channels, hidden), lambda e: (e, 0, 0))
    return pl.pallas_call(
        expert_kernel,
        grid=(experts,),
        out_shape=[
            jax.ShapeDtypeStruct(inputs.shape, jnp.bfloat16),
            jax.ShapeDtypeStruct((experts, 2, pieces, channels, 128), jnp.float32),
        ],
        in_specs=[tok, tok, weight, weight],
        out_specs=[tok, pl.BlockSpec((None, 2, pieces, channels, 128), lambda e: (e, 0, 0, 0, 0))],
        compiler_params=pltpu.CompilerParams(vmem_limit_bytes=48 * 1024 * 1024),
    )(inputs, grads, w_in, w_out_t)

def assemble_kernel(slot_ref, dense_ref, ret_ref, out_ref):
    per_row = dense_ref.shape[2] // ret_ref.shape[2]
    width = ret_ref.shape[2]
    for b in range(dense_ref.shape[0] * per_row):
        h, k = b // per_row, b % per_row
        piece = dense_ref[h, :, k * width:(k + 1) * width].astype(jnp.float32)
        piece = piece + ret_ref[slot_ref[b]].astype(jnp.float32)
        out_ref[h, :, k * width:(k + 1) * width] = piece.astype(out_ref.dtype)


def assemble(slot_of, dense_t, ret):
    return pl.pallas_call(
        assemble_kernel,
        out_shape=jax.ShapeDtypeStruct(dense_t.shape, dense_t.dtype),
        in_specs=[
            pl.BlockSpec(memory_space=pltpu.SMEM),
            pl.BlockSpec(memory_space=pltpu.VMEM),
            pl.BlockSpec(memory_space=pltpu.VMEM),
        ],
        out_specs=pl.BlockSpec(memory_space=pltpu.VMEM),
    )(slot_of, dense_t, ret)


def place_kernel(source_ref, filled_ref, src_ref, out_ref):
    width = out_ref.shape[2]
    per_row = src_ref.shape[2] // width
    for s in range(out_ref.shape[0]):
        b = source_ref[s]
        row = src_ref[b // per_row]
        k = b % per_row
        piece = row[:, 0:width]
        for j in range(1, per_row):
            piece = jnp.where(k == j, row[:, j * width:(j + 1) * width], piece)
        out_ref[s] = jnp.where(filled_ref[s] > 0, piece, jnp.zeros_like(piece))


def place(block_of_slot, filled, src_t, width):
    slots = block_of_slot.shape[0]
    return pl.pallas_call(
        place_kernel,
        out_shape=jax.ShapeDtypeStruct((slots, src_t.shape[1], width), src_t.dtype),
        in_specs=[
            pl.BlockSpec(memory_space=pltpu.SMEM),
            pl.BlockSpec(memory_space=pltpu.SMEM),
            pl.BlockSpec(memory_space=pltpu.VMEM),
        ],
        out_specs=pl.BlockSpec(memory_space=pltpu.VMEM),
    )(block_of_slot, filled, src_t)


def gelu_slope(values):
    return (
        0.5 * (1.0 + lax.erf(values * 0.7071067811865476))
        + values * jnp.exp(-0.5 * values * values) * 0.3989422804014327
    )


def depthwise(padded, kernel):
    row_count = padded.shape[1] - 6
    col_count = padded.shape[2] - 6
    summed = jnp.zeros((padded.shape[0], row_count, col_count, padded.shape[3]), jnp.float32)
    for row_off in range(7):
        for col_off in range(7):
            window = padded[:, row_off : row_off + row_count, col_off : col_off + col_count, :]
            summed = summed + window.astype(jnp.float32) * kernel[row_off, col_off]
    return summed


def widen(picture):
    return jnp.pad(picture, ((0, 0), (0, 0), (3, 3), (0, 0)))


def dense_block(images, smoothed, ln_gain, w_expand, w_reduce):
    channels = images.shape[-1]
    channel_mean = jnp.mean(smoothed, axis=-1, keepdims=True)
    centered = smoothed - channel_mean
    variance = jnp.mean(centered * centered, axis=-1, keepdims=True)
    normed = (centered * lax.rsqrt(variance + 1e-06) * ln_gain).astype(jnp.bfloat16)
    flat_normed = normed.reshape(-1, channels)
    expanded = jnp.dot(flat_normed, w_expand, preferred_element_type=jnp.float32)
    active = jax.nn.gelu(expanded, approximate=False).astype(jnp.bfloat16)
    reduced = jnp.dot(active, w_reduce, preferred_element_type=jnp.float32)
    dense_out = images.reshape(-1, channels).astype(jnp.float32) + reduced
    return dense_out.astype(jnp.bfloat16).reshape(images.shape)


def expert_pass(inputs, grads_in, w_in, w_out):
    pre_act = jnp.dot(inputs, w_in, preferred_element_type=jnp.float32)
    hidden = jax.nn.gelu(pre_act, approximate=False).astype(jnp.bfloat16)
    outputs = jnp.dot(hidden, w_out, preferred_element_type=jnp.float32).astype(jnp.bfloat16)
    grad_out = jnp.dot(hidden.T, grads_in, preferred_element_type=jnp.float32)
    back_prop = jnp.dot(grads_in, w_out.T, preferred_element_type=jnp.float32)
    scaled = (back_prop * gelu_slope(pre_act)).astype(jnp.bfloat16)
    grad_in = jnp.dot(inputs.T, scaled, preferred_element_type=jnp.float32)
    return (outputs, grad_in, grad_out)


def body(images, cotangent, labels, dw_kernel, ln_gain, w_expand, w_reduce, exp_in, exp_out):
    channels = images.shape[-1]
    padded = with_halo(images, (("lat", 1),), 3)
    smoothed = depthwise(widen(padded), dw_kernel)
    dense_out = dense_block(images, smoothed, ln_gain, w_expand, w_reduce)
    rows, width = images.shape[1], images.shape[2]
    per_row = width // BLOCK

    def to_blocks(pixels):
        pixels = pixels.reshape(rows, per_row, BLOCK, channels)
        return jnp.transpose(pixels, (0, 1, 3, 2)).reshape(rows * per_row, channels, BLOCK)

    flat_labels = labels.reshape(-1)
    members = (flat_labels[:, None] == jnp.arange(EXPERTS, dtype=jnp.int32)[None, :]).astype(
        jnp.int32
    )
    before = jnp.sum(jnp.cumsum(members, axis=0) * members, axis=1) - 1
    slot_of = flat_labels * CAP + before
    placer = jnp.arange(EXPERTS * CAP, dtype=jnp.int32)[:, None] == slot_of[None, :]
    block_of_slot = jnp.argmax(placer, axis=1)
    filled = jnp.any(placer, axis=1)[:, None, None]
    source = block_of_slot.astype(jnp.int32)
    flags = filled.reshape(-1).astype(jnp.int32)
    keep_all = jnp.ones_like(flags)
    dense_t = jnp.transpose(dense_out.reshape(rows, width, channels), (0, 2, 1))
    cot_t = jnp.transpose(cotangent.reshape(rows, width, channels), (0, 2, 1))
    outgoing = place(source, keep_all, dense_t, BLOCK).reshape(EXPERTS, CAP, channels, BLOCK)
    outgoing_grads = place(source, flags, cot_t, BLOCK).reshape(EXPERTS, CAP, channels, BLOCK)
    groups = lax.axis_size("exp")
    local = EXPERTS // groups
    by_group = (groups, local, CAP, channels, BLOCK)
    arrived, arrived_grads = (
        lax.all_to_all(outgoing.reshape(by_group), "exp", split_axis=0, concat_axis=0, tiled=True),
        lax.all_to_all(outgoing_grads.reshape(by_group), "exp", split_axis=0, concat_axis=0, tiled=True),
    )
    results, flat = run_experts(arrived, arrived_grads, exp_in, jnp.transpose(exp_out, (0, 2, 1)))
    returned = lax.all_to_all(results, "exp", split_axis=0, concat_axis=0, tiled=True)
    grad_in, grad_out_t = tree_allreduce(flat.reshape(-1, 128), local, channels, exp_in.shape[2])
    grad_out = jnp.transpose(grad_out_t, (0, 2, 1))
    out_t = assemble(slot_of.astype(jnp.int32), dense_t, returned.reshape(EXPERTS * CAP, channels, BLOCK))
    output = jnp.transpose(out_t, (0, 2, 1)).reshape(dense_out.shape)
    return (output, grad_in, grad_out)


def solution(mesh):
    in_specs = (
        P(("dp", "exp"), "lat", None, None),
        P(("dp", "exp"), "lat", None, None),
        P(("dp", "exp"), "lat", None, None),
        P(),
        P(),
        P(),
        P(),
        P("exp", None, None),
        P("exp", None, None),
    )
    out_specs = (P(("dp", "exp"), "lat", None, None), P("exp", None, None), P("exp", None, None))
    return jax.shard_map(body, mesh=mesh, in_specs=in_specs, out_specs=out_specs, check_vma=False)
```
